512 devices in a mesh: gx: 32 (over z, core), gy: 4 (over y), gz: 4 (over x).
Axes of the slice: x: 4, y: 4, z: 16, core: 2. Of those that a mesh axis runs over, the one named last changes fastest.
Arguments:
- right_side: float32 [512, 256, 512], P('gx', 'gy', 'gz'), may hold values from -18 to 18
- inv_density: float32 [512, 256, 512], P('gx', 'gy', 'gz'), may hold values from 0.5 to 2
- active: int32 [512, 256, 512], P('gx', 'gy', 'gz'), may hold values 0 or 1
Outputs:
- solution_field: float32 [512, 256, 512], P('gx', 'gy', 'gz')
- residual: float32 [512, 256, 512], P('gx', 'gy', 'gz')
The draws below stay inside these ranges and needn't reach their ends.
All inputs are finite; a program needn't handle non-finite values. No bound on the sum of `active` on one device may be relied on, other than what follows from the above.
Results may differ from the reference program's by a relative error of at most 0.0003.
Values sent between devices are 32-bit elements; how exact they have to be, the bound alone decides.
A program may use at most 64 MiB of HBM per device.

```python
import math
import jax
import jax.numpy as jnp
from jax import lax

STEPS = 6
NX = 512
NY = 256
NZ = 512


def draw_right_side(key, part):
    x_position = lax.broadcasted_iota(jnp.float32, (NX, NY, NZ), 0)
    fraction = x_position / (NX - 1.0)
    rough_part = jnp.clip(jax.random.normal(key, (NX, NY, NZ), jnp.float32), -6.0, 6.0)
    return rough_part * (1.0 + 2.0 * fraction)


def set_ends(entries, stream_key, least, high):
    longest = entries.shape.index(max(entries.shape))
    spots = []
    for shift in (0, 1):
        where = [jax.random.randint(jax.random.fold_in(stream_key, axis), (), 0, length) for axis, length in enumerate(entries.shape)]
        where[longest] = (where[longest] + shift) % entries.shape[longest]
        spots.append(tuple(where))
    return entries.at[spots[0]].set(least).at[spots[1]].set(high)


def block_levels(stream_key, dims, cuts, least, top_value):
    loudness, own = 1.0, jax.random.fold_in(stream_key, 6)
    for position, shards_of in cuts:
        heights = jnp.exp(jax.random.uniform(jax.random.fold_in(own, position), (shards_of,), jnp.float32, least / len(cuts), top_value / len(cuts)))
        loudness = loudness * jnp.repeat(heights, dims[position] // shards_of).reshape([-1 if axis == position else 1 for axis in range(len(dims))])
    return loudness


def setup_inputs(seed: int = 0) -> dict:
    key_list = jax.random.split(jax.random.key(seed), 4)
    right_side = draw_right_side(jax.random.fold_in(key_list[3], 71), 0)
    inv_density = jnp.clip(jnp.exp(math.log(2.0) - 1.3862944 * jax.random.uniform(key_list[1], (NX, NY, NZ), jnp.float32) ** block_levels(key_list[1], (NX, NY, NZ), ((0, 32), (1, 4), (2, 4)), -0.2, 0.2)), 0.5, 2.0)
    active = set_ends((jax.random.randint(key_list[2], (NX, NY, NZ), 0, 4) < 3).astype(jnp.int32), jax.random.fold_in(key_list[2], 1), 0, 1)
    return {"right_side": right_side, "inv_density": inv_density, "active": active}


basis_shift = 7.0
basis_scale = 7.0
NEIGHBOURS = ((2, 1, 1), (0, 1, 1), (1, 2, 1), (1, 0, 1), (1, 1, 2), (1, 1, 0))

def shifted(field, offset):
    extent = field.shape
    return field[offset[0]:extent[0] - 2 + offset[0], offset[1]:extent[1] - 2 + offset[1], offset[2]:extent[2] - 2 + offset[2]]

def apply_valid(vector_pad, weight_pad):
    center_weight = shifted(weight_pad, (1, 1, 1))
    center_value = shifted(vector_pad, (1, 1, 1))
    diagonal = jnp.zeros_like(center_value)
    beside = jnp.zeros_like(center_value)
    for offset in NEIGHBOURS:
        other_weight = shifted(weight_pad, offset)
        other_value = shifted(vector_pad, offset)
        liquid_side = other_weight > 0.0
        denominator = jnp.where(liquid_side, center_weight + other_weight, 1.0)
        face_value = jnp.where(liquid_side, 2.0 * center_weight * other_weight / denominator, center_weight)
        diagonal = diagonal + face_value
        beside = beside + face_value * other_value
    return diagonal * center_value - beside

def next_basis(image_field, previous):
    return (image_field - basis_shift * previous) / basis_scale

def least_squares(triangle):
    column_count = triangle.shape[1] - 1
    row_ids = lax.broadcasted_iota(jnp.int32, (column_count + 1, column_count), 0)
    col_ids = lax.broadcasted_iota(jnp.int32, (column_count + 1, column_count), 1)
    change = jnp.where(row_ids == col_ids, basis_shift, 0.0) + jnp.where(row_ids == col_ids + 1, basis_scale, 0.0)
    change = change.astype(triangle.dtype)
    hess = jnp.dot(triangle, change, precision=lax.Precision.HIGHEST)
    target = triangle[:, 0]
    for pivot_index in range(column_count):
        first_value = hess[pivot_index, pivot_index]
        second_value = hess[pivot_index + 1, pivot_index]
        radius = jnp.sqrt(first_value * first_value + second_value * second_value)
        cosine = first_value / radius
        sine_value = second_value / radius
        upper_row = cosine * hess[pivot_index] + sine_value * hess[pivot_index + 1]
        lower_row = cosine * hess[pivot_index + 1] - sine_value * hess[pivot_index]
        hess = hess.at[pivot_index].set(upper_row).at[pivot_index + 1].set(lower_row)
        upper_target = cosine * target[pivot_index] + sine_value * target[pivot_index + 1]
        lower_target = cosine * target[pivot_index + 1] - sine_value * target[pivot_index]
        target = target.at[pivot_index].set(upper_target).at[pivot_index + 1].set(lower_target)
    solved = [None] * column_count
    for row_index in reversed(range(column_count)):
        running = target[row_index]
        for column_index in range(row_index + 1, column_count):
            running = running - hess[row_index, column_index] * solved[column_index]
        solved[row_index] = running / hess[row_index, row_index]
    coefficients = jnp.stack(solved)
    first_unit = jnp.where(lax.broadcasted_iota(jnp.int32, (column_count + 1,), 0) == 0, 1.0, 0.0).astype(triangle.dtype)
    leftover = first_unit - jnp.dot(change, coefficients, precision=lax.Precision.HIGHEST)
    return (coefficients, leftover)

def reference(right_side, inv_density, active):
    liquid = active.astype(jnp.float32)
    weight = inv_density * liquid
    weight_pad = jnp.pad(weight, 1)
    basis_list = [right_side * liquid]
    for power_index in range(STEPS):
        image_field = apply_valid(jnp.pad(basis_list[-1], 1), weight_pad)
        basis_list.append(next_basis(image_field, basis_list[-1]))
    gram_matrix = jnp.zeros((STEPS + 1, STEPS + 1), jnp.float32)
    for row_index in range(STEPS + 1):
        for column_index in range(row_index + 1):
            product = jnp.sum(basis_list[row_index] * basis_list[column_index])
            gram_matrix = gram_matrix.at[row_index, column_index].set(product).at[column_index, row_index].set(product)
    triangle = jnp.linalg.cholesky(gram_matrix).T
    coefficients, leftover = least_squares(triangle)
    solution_field = jnp.zeros_like(right_side)
    for power_index in range(STEPS):
        solution_field = solution_field + coefficients[power_index] * basis_list[power_index]
    residual = jnp.zeros_like(right_side)
    for power_index in range(STEPS + 1):
        residual = residual + leftover[power_index] * basis_list[power_index]
    return (solution_field, residual)
```

```python
import jax
import jax.numpy as jnp
from jax import lax
from jax.experimental import pallas as pl
from jax.experimental.pallas import tpu as pltpu
from jax.sharding import PartitionSpec as P

STEPS = 6
MOMENTS = 2 * STEPS + 1
SHIFT = 7.0
MESH = pl.DeviceIdType.MESH
F32 = jnp.float32
LANES = 128
WEIGHT = 7


def face_pair(here, other):
    liquid = other > 0.0
    total = jnp.where(liquid, here + other, 1.0)
    shared = 2.0 * here * other / total
    return jnp.where(liquid, shared, here), jnp.where(liquid, shared, 0.0)


def make_kernel(shape, counts):
    nx, ny, nz = shape
    gxn, gyn, gzn = counts
    tiles = ny // 8
    pitch = ny + 16
    halves = nx * tiles * 2 // LANES
    per_half = nx // halves
    stride = 2 * tiles
    plane = 2 * gyn * gzn
    chips = gxn // 2

    def rows_of(slab):
        return pl.ds(pl.multiple_of(slab * pitch + 8, 8), ny)

    def kernel(rs, inv, act, sol, res, rs_v, inv_v, act_v, B, YS, YG, ZS, ZG,
               HX, HY, HZM, HZP, D, MU, SA, RA, SB, RB, OS, OR,
               in_sem, out_sem, xs, xr, ys, yr, zs, zr, a_send, a_recv, b_send, b_recv):
        gx, gy, gz = lax.axis_index("gx"), lax.axis_index("gy"), lax.axis_index("gz")
        chip, core = gx // 2, gx % 2
        pos = (gx, gy, gz)

        loads = [
            pltpu.make_async_copy(src, dst, in_sem.at[i])
            for i, (src, dst) in enumerate(((rs, rs_v), (inv, inv_v), (act, act_v)))
        ]
        for copy in loads:
            copy.start()

        low = (gx > 0, gy > 0, gz > 0)
        high = (gx < gxn - 1, gy < gyn - 1, gz < gzn - 1)

        def plane_peer(d):
            t = (core + 2 * (gy + gyn * gz) + d) % plane
            return {"gx": 2 * chip + t % 2, "gy": (t // 2) % gyn, "gz": t // (2 * gyn)}

        def chip_peer(d):
            return {"gx": 2 * ((chip + d) % chips) + core}

        barrier = pltpu.get_barrier_semaphore()

        def greet(device):
            pl.semaphore_signal(barrier, inc=1, device_id=device, device_id_type=MESH)

        @pl.when((core == 0) & low[0])
        def _():
            greet({"gx": gx - 1})

        @pl.when((core == 1) & high[0])
        def _():
            greet({"gx": gx + 1})

        @pl.loop(1, plane)
        def _(d):
            greet(plane_peer(d))

        @pl.loop(1, chips)
        def _(d):
            greet(chip_peer(d))

        @pl.when(jnp.logical_not(low[0]))
        def _():
            for k in range(8):
                if k != 6:
                    B[k, pl.ds(8, ny), :] = jnp.zeros((ny, LANES), F32)

        @pl.when(jnp.logical_not(high[0]))
        def _():
            for k in range(8):
                if k != 6:
                    B[k, pl.ds((nx + 1) * pitch + 8, ny), :] = jnp.zeros((ny, LANES), F32)

        for side, there in ((0, low), (1, high)):
            @pl.when(jnp.logical_not(there[1]))
            def _():
                for k in range(8):
                    if k != 6:
                        YG[k, side] = jnp.zeros((nx, LANES), F32)

            @pl.when(jnp.logical_not(there[2]))
            def _():
                for k in range(8):
                    if k != 6:
                        ZG[k, side] = jnp.zeros((halves, 8, LANES), F32)

        for x in range(nx):
            B[WEIGHT, pl.ds((x + 1) * pitch + ny + 8, 8), :] = jnp.zeros((8, LANES), F32)

        across = ((core == 0) & low[0]) | ((core == 1) & high[0])
        pl.semaphore_wait(barrier, plane + chips - 2 + across.astype(jnp.int32))

        lane = lax.broadcasted_iota(jnp.int32, (8, LANES), 1)
        lane_s = lax.broadcasted_iota(jnp.int32, (ny, LANES), 1)
        first, last = lane_s == 0, lane_s == LANES - 1
        odd = lane % 2 == 1

        def x_copy(k, side):
            src, dst, to = ((1, nx + 1, gx - 1), (nx, 0, gx + 1))[side]
            return pltpu.make_async_remote_copy(
                B.at[k, rows_of(src)], B.at[k, rows_of(dst)], xs.at[k, side], xr.at[k, 1 - side],
                device_id={"gx": to}, device_id_type=MESH)

        def y_copy(k, side):
            return pltpu.make_async_remote_copy(
                YS.at[k, side], YG.at[k, 1 - side], ys.at[k, side], yr.at[k, 1 - side],
                device_id={"gy": gy + 2 * side - 1}, device_id_type=MESH)

        def z_copy(k, side):
            return pltpu.make_async_remote_copy(
                ZS.at[k], ZG.at[k, 1 - side], zs.at[k, side], zr.at[k, 1 - side],
                device_id={"gz": gz + 2 * side - 1}, device_id_type=MESH)

        copies = (x_copy, y_copy, z_copy)

        def on_sides(act_on, axes=(0, 1, 2)):
            for axis in axes:
                for side, there in ((0, low), (1, high)):
                    @pl.when(there[axis])
                    def _():
                        act_on(copies[axis], side)

        def y_pack(k):
            for side, row in ((0, 0), (1, ny - 1)):
                YS[k, side] = B[k, pl.ds(pitch + 8 + row, nx, stride=pitch), :]

        def y_unpack(k):
            B[k, pl.ds(pitch + 7, nx, stride=pitch), :] = YG[k, 0]
            B[k, pl.ds(pitch + 8 + ny, nx, stride=pitch), :] = YG[k, 1]

        def pack_part(slab, xi):
            ends = jnp.where(first | last, slab, 0.0)
            part = ends[0:8]
            for t in range(1, tiles):
                part = part + pltpu.roll(ends[8 * t : 8 * t + 8], 2 * t, 1)
            return pltpu.roll(part, stride * xi, 1)

        def ghost_columns(ghost, xi):
            base = pltpu.roll(ghost, (LANES - stride * xi) % LANES, 1)
            parts = [base] + [pltpu.roll(base, LANES - 2 * t, 1) for t in range(1, tiles)]
            return jnp.concatenate(parts, axis=0)

        def z_ghost(k, xo):
            return jnp.where(odd, ZG[k, 0, xo], ZG[k, 1, xo])

        def z_shift(slab, columns):
            lower = pltpu.roll(jnp.where(last, columns, slab), 1, 1)
            upper = pltpu.roll(jnp.where(first, columns, slab), LANES - 1, 1)
            return lower, upper

        def fold(slab):
            total = slab[0:8]
            for t in range(1, tiles):
                total = total + slab[8 * t : 8 * t + 8]
            return total

        for copy in loads:
            copy.wait()

        mu0 = jnp.zeros((8, LANES), F32)
        for xo in range(halves):
            def first_pass(xi, carry):
                mu, wp, bp = carry
                x = xo * per_half + xi
                liquid = act_v[x].astype(F32)
                w, b = inv_v[x] * liquid, rs_v[x] * liquid
                B[WEIGHT, rows_of(x + 1), :] = w
                B[0, rows_of(x + 1), :] = b
                return mu + fold(b * b), wp + pack_part(w, xi), bp + pack_part(b, xi)

            zero = jnp.zeros((8, LANES), F32)
            mu0, wp, bp = lax.fori_loop(0, per_half, first_pass, (mu0, zero, zero))
            ZS[WEIGHT, xo] = wp
            ZS[0, xo] = bp
        MU[0] = mu0
        y_pack(WEIGHT)
        y_pack(0)
        on_sides(lambda copy, side: copy(WEIGHT, side).start())
        on_sides(lambda copy, side: copy(0, side).start())

        on_sides(lambda copy, side: copy(WEIGHT, 1 - side).wait_recv())
        y_unpack(WEIGHT)
        scale = -1.0 / SHIFT
        for xo in range(halves):
            def face_pass(xi, _):
                x = xo * per_half + xi
                row = (x + 1) * pitch + 8
                center = B[WEIGHT, rows_of(x + 1), :]
                columns = ghost_columns(z_ghost(WEIGHT, xo), xi)
                lower, upper = z_shift(center, columns)
                total = jnp.zeros((ny, LANES), F32)
                for other, keep, at in (
                    (B[WEIGHT, rows_of(x + 2), :], HX, pl.ds(pl.multiple_of((x + 1) * ny, 8), ny)),
                    (B[WEIGHT, rows_of(x), :], HX, pl.ds(pl.multiple_of(x * ny, 8), ny)),
                    (B[WEIGHT, pl.ds(row + 1, ny), :], HY, pl.ds(row + 1, ny)),
                    (B[WEIGHT, pl.ds(row - 1, ny), :], HY, pl.ds(row, ny)),
                    (upper, HZP, pl.ds(pl.multiple_of(x * ny, 8), ny)),
                    (lower, HZM, pl.ds(pl.multiple_of(x * ny, 8), ny)),
                ):
                    face, shared = face_pair(center, other)
                    total = total + face
                    keep[at, :] = shared * scale
                D[pl.ds(pl.multiple_of(x * ny, 8), ny), :] = total * (1.0 / SHIFT) - 1.0
                return 0

            lax.fori_loop(0, per_half, face_pass, 0)

        @pl.loop(0, STEPS)
        def _(k):
            on_sides(lambda copy, side: copy(k, 1 - side).wait_recv())
            y_unpack(k)
            odd_mu = jnp.zeros((8, LANES), F32)
            even_mu = jnp.zeros((8, LANES), F32)
            for xo in range(halves):
                ghost = z_ghost(k, xo)

                def step(xi, carry):
                    mixed, square, packed = carry
                    x = xo * per_half + xi
                    row = (x + 1) * pitch + 8
                    flat = pl.ds(pl.multiple_of(x * ny, 8), ny)
                    above = pl.ds(pl.multiple_of((x + 1) * ny, 8), ny)
                    center = B[k, rows_of(x + 1), :]
                    lower, upper = z_shift(center, ghost_columns(ghost, xi))
                    image = D[flat, :] * center
                    image = image + HX[above, :] * B[k, rows_of(x + 2), :]
                    image = image + HX[flat, :] * B[k, rows_of(x), :]
                    image = image + HY[pl.ds(row + 1, ny), :] * B[k, pl.ds(row + 1, ny), :]
                    image = image + HY[pl.ds(row, ny), :] * B[k, pl.ds(row - 1, ny), :]
                    image = image + HZP[flat, :] * upper
                    image = image + HZM[flat, :] * lower
                    B[k + 1, rows_of(x + 1), :] = image
                    return (mixed + fold(center * image), square + fold(image * image),
                            packed + pack_part(image, xi))

                odd_mu, even_mu, packed = lax.fori_loop(
                    0, per_half, step, (odd_mu, even_mu, jnp.zeros((8, LANES), F32)))
                ZS[k + 1, xo] = packed
            MU[2 * k + 1] = odd_mu
            MU[2 * k + 2] = even_mu

            @pl.when(k < STEPS - 1)
            def _():
                y_pack(k + 1)
                on_sides(lambda copy, side: copy(k + 1, side).start())

        for spare in range(MOMENTS, 16):
            MU[spare] = jnp.zeros((8, LANES), F32)
        local = jnp.sum(jnp.sum(MU[...], axis=1), axis=1, keepdims=True)
        diagonal = (lax.broadcasted_iota(jnp.int32, (16, LANES), 0)
                    == lax.broadcasted_iota(jnp.int32, (16, LANES), 1))
        row = jnp.sum(jnp.where(diagonal, jnp.broadcast_to(local, (16, LANES)), 0.0), axis=0, keepdims=True)

        def all_sum(row, staged, landed, send, recv, peers, me, peer):
            staged[...] = row
            landed[me] = row

            @pl.loop(1, peers)
            def _(d):
                pltpu.make_async_remote_copy(
                    staged, landed.at[me], send, recv, device_id=peer(d), device_id_type=MESH).start()

            whole = landed.at[pl.ds(0, peers - 1)]
            pltpu.make_async_copy(whole, whole, recv).wait()
            total = landed[0]
            for i in range(1, peers):
                total = total + landed[i]
            return total

        row = all_sum(row, SA, RA, a_send, a_recv, plane, core + 2 * (gy + gyn * gz), plane_peer)
        row = all_sum(row, SB, RB, b_send, b_recv, chips, chip, chip_peer)

        spread = jnp.broadcast_to(row, (8, LANES))
        mu = [jnp.broadcast_to(spread[:, i : i + 1], (8, LANES)) for i in range(MOMENTS)]
        size = STEPS + 1
        gram = [[mu[i + j] for j in range(size)] for i in range(size)]
        side = [jnp.full((8, LANES), (-1.0) ** i, F32) for i in range(size)]
        inverse = []
        for p in range(size):
            inverse.append(1.0 / gram[p][p])
            for i in range(p + 1, size):
                factor = gram[p][i] * inverse[p]
                for j in range(i, size):
                    gram[i][j] = gram[i][j] - factor * gram[p][j]
                side[i] = side[i] - factor * side[p]
        solved = [None] * size
        for i in reversed(range(size)):
            running = side[i]
            for j in range(i + 1, size):
                running = running - gram[i][j] * solved[j]
            solved[i] = running * inverse[i]
        norm = solved[0]
        for i in range(1, size):
            norm = norm - solved[i] if i % 2 else norm + solved[i]
        norm = 1.0 / norm
        leftover = [value * norm for value in solved]
        scaled = [None] * STEPS
        scaled[STEPS - 1] = -leftover[STEPS]
        for i in reversed(range(STEPS - 1)):
            scaled[i] = -leftover[i + 1] - scaled[i + 1]
        for i in range(STEPS):
            MU[i] = scaled[i] * (1.0 / SHIFT)
        for i in range(size):
            MU[8 + i] = leftover[i]

        chunk = 4

        def out_copies(part):
            at = pl.ds(part * chunk, chunk)
            return [pltpu.make_async_copy(src.at[at], dst.at[at], out_sem.at[i, part])
                    for i, (src, dst) in enumerate(((OS, sol), (OR, res)))]

        @pl.loop(0, nx // chunk)
        def _(part):
            @pl.loop(0, chunk)
            def _(within):
                x = part * chunk + within
                for t in range(tiles):
                    at = pl.ds(pl.multiple_of((x + 1) * pitch + 8 + 8 * t, 8), 8)
                    value = B[0, at, :]
                    s, r = MU[0] * value, MU[8] * value
                    for i in range(1, size):
                        value = B[i, at, :]
                        if i < STEPS:
                            s = s + MU[i] * value
                        r = r + MU[8 + i] * value
                    OS[x, pl.ds(8 * t, 8), :] = s
                    OR[x, pl.ds(8 * t, 8), :] = r

            for copy in out_copies(part):
                copy.start()

        for k in tuple(range(STEPS)) + (WEIGHT,):
            on_sides(lambda copy, side: copy(k, side).wait_send())
        for landed, send, peers in ((RA, a_send, plane), (RB, b_send, chips)):
            whole = landed.at[pl.ds(0, peers - 1)]
            pltpu.make_async_copy(whole, whole, send).wait()

        @pl.loop(0, nx // chunk)
        def _(part):
            for copy in out_copies(part):
                copy.wait()

    scratch = [
        pltpu.VMEM((nx, ny, nz), F32), pltpu.VMEM((nx, ny, nz), F32), pltpu.VMEM((nx, ny, nz), jnp.int32),
        pltpu.VMEM((8, (nx + 2) * pitch, LANES), F32),
        pltpu.VMEM((8, 2, nx, LANES), F32), pltpu.VMEM((8, 2, nx, LANES), F32),
        pltpu.VMEM((8, halves, 8, LANES), F32), pltpu.VMEM((8, 2, halves, 8, LANES), F32),
        pltpu.VMEM(((nx + 1) * ny, LANES), F32), pltpu.VMEM(((nx + 2) * pitch, LANES), F32),
        pltpu.VMEM((nx * ny, LANES), F32), pltpu.VMEM((nx * ny, LANES), F32),
        pltpu.VMEM((nx * ny, LANES), F32),
        pltpu.VMEM((16, 8, LANES), F32),
        pltpu.VMEM((1, LANES), F32), pltpu.VMEM((plane, 1, LANES), F32),
        pltpu.VMEM((1, LANES), F32), pltpu.VMEM((chips, 1, LANES), F32),
        pltpu.VMEM((nx, ny, nz), F32), pltpu.VMEM((nx, ny, nz), F32),
        pltpu.SemaphoreType.DMA((3,)), pltpu.SemaphoreType.DMA((2, 4)),
    ] + [pltpu.SemaphoreType.DMA((8, 2))] * 6 + [pltpu.SemaphoreType.DMA] * 4
    return kernel, scratch


def solution(mesh):
    counts = tuple(mesh.shape[axis] for axis in ("gx", "gy", "gz"))

    def on_device(right_side, inv_density, active):
        kernel, scratch = make_kernel(right_side.shape, counts)
        field = jax.ShapeDtypeStruct(right_side.shape, F32)
        return pl.pallas_call(
            kernel,
            out_shape=(field, field),
            in_specs=[pl.BlockSpec(memory_space=pl.ANY)] * 3,
            out_specs=(pl.BlockSpec(memory_space=pl.ANY),) * 2,
            scratch_shapes=scratch,
            compiler_params=pltpu.CompilerParams(collective_id=0, has_side_effects=True),
        )(right_side, inv_density, active)

    placed = P("gx", "gy", "gz")
    return jax.shard_map(
        on_device, mesh=mesh, in_specs=(placed,) * 3, out_specs=(placed,) * 2, check_vma=False)
```

```python
import jax
import jax.numpy as jnp
from jax import lax
from jax.experimental import pallas as pl
from jax.experimental.pallas import tpu as pltpu
from jax.sharding import PartitionSpec as P

STEPS = 6
SIZE = STEPS + 1
MOMENTS = 2 * STEPS + 1
SHIFT = 7.0
MESH = pl.DeviceIdType.MESH
F32 = jnp.float32
LANES = 128
WEIGHT = 7
SLOTS = tuple(range(STEPS)) + (WEIGHT,)


def scaled_face(here, other):
    total = jnp.where(other > 0.0, here + other, 1.0)
    return (here * (-2.0 / SHIFT)) * other / total


def tree(values):
    values = list(values)
    while len(values) > 1:
        values = [values[i] + values[i + 1] if i + 1 < len(values) else values[i]
                  for i in range(0, len(values), 2)]
    return values[0]


class Sums:
    def __init__(self, count=4):
        self.parts, self.turn = [None] * count, 0

    def add(self, value):
        held = self.parts[self.turn]
        self.parts[self.turn] = value if held is None else held + value
        self.turn = (self.turn + 1) % len(self.parts)

    def total(self):
        return tree([part for part in self.parts if part is not None])


def make_kernel(shape, counts):
    nx, ny, nz = shape
    gxn, gyn, gzn = counts
    tiles = ny // 8
    pitch = ny + 16
    halves = nx * tiles * 2 // LANES
    plane = 2 * gyn * gzn
    chips = gxn // 2
    chunk = 4

    def row(x, t=0):
        return (x + 1) * pitch + 8 + 8 * t

    def at(x, t):
        return pl.ds(row(x, t), 8)

    def flat(x, t):
        return pl.ds(x * ny + 8 * t, 8)

    def slab(x):
        return pl.ds(row(x), ny)

    def place(x, t):
        j = x * tiles + t
        return j // (LANES // 2), 2 * (j % (LANES // 2))

    def turn(value, amount):
        amount %= LANES
        return pltpu.roll(value, amount, 1) if amount else value

    def is_rim(x, t):
        return x in (0, nx - 1) or t in (0, tiles - 1)

    every = [(x, t) for x in range(nx) for t in range(tiles)]
    inner = [xt for xt in every if not is_rim(*xt)]
    caps = [xt for xt in every if xt[0] in (0, nx - 1)]
    sides_y = [xt for xt in every if is_rim(*xt) and xt[0] not in (0, nx - 1)]

    def kernel(rs, inv, act, sol, res, rs_v, inv_v, act_v, B, YS, YG, ZS, ZG,
               HX, HY, HYG, HZM, HZP, FP, D, MU, SA, RA, SB, RB, OS, OR,
               in_sem, out_sem, xs, xr, ys, yr, zs, zr, a_send, a_recv, b_send, b_recv, far):
        gx, gy, gz = lax.axis_index("gx"), lax.axis_index("gy"), lax.axis_index("gz")
        chip, core = gx // 2, gx % 2
        nil = gx // 4096

        def near(start):
            return pl.ds(nil + start, 8)

        def load_copies(part):
            where = pl.ds(part * chunk, chunk)
            return [pltpu.make_async_copy(src.at[where], dst.at[where], in_sem.at[i, part])
                    for i, (src, dst) in enumerate(((rs, rs_v), (inv, inv_v), (act, act_v)))]

        for part in range(nx // chunk):
            for copy in load_copies(part):
                copy.start()

        low = (gx > 0, gy > 0, gz > 0)
        high = (gx < gxn - 1, gy < gyn - 1, gz < gzn - 1)
        names = ("gx", "gy", "gz")
        pos = (gx, gy, gz)

        def chip_peer(d):
            return {"gx": (gx + 2 * d) % gxn}

        barrier = pltpu.get_barrier_semaphore()

        def greet(semaphore, device):
            pl.semaphore_signal(semaphore, inc=1, device_id=device, device_id_type=MESH)

        present = 2
        for axis in range(3):
            for there, step in ((low, -1), (high, 1)):
                present = present + there[axis].astype(jnp.int32)

                @pl.when(there[axis])
                def _():
                    greet(barrier, {names[axis]: pos[axis] + step})

        greet(barrier, chip_peer(1))
        greet(barrier, chip_peer(chips - 1))

        for side, there in ((0, low), (1, high)):
            @pl.when(jnp.logical_not(there[0]))
            def _():
                for k in SLOTS:
                    B[k, slab((-1, nx)[side]), :] = jnp.zeros((ny, LANES), F32)

            @pl.when(jnp.logical_not(there[1]))
            def _():
                for k in SLOTS:
                    YG[k, side] = jnp.zeros((nx, LANES), F32)

            @pl.when(jnp.logical_not(there[2]))
            def _():
                for k in SLOTS:
                    ZG[k, side] = jnp.zeros((halves, 8, LANES), F32)

        none = jnp.zeros((nx, LANES), F32)
        for k in SLOTS:
            B[k, pl.ds(row(0) - 1, nx, stride=pitch), :] = none
            B[k, pl.ds(row(0) + ny, nx, stride=pitch), :] = none
        HY[pl.ds(row(0) + ny, nx, stride=pitch), :] = none
        for spare in (0, 14, 15):
            MU[spare] = jnp.zeros((8, LANES), F32)

        lane = lax.broadcasted_iota(jnp.int32, (8, LANES), 1)
        first, last = lane == 0, lane == LANES - 1
        ends = first | last
        odd = lane % 2 == 1

        def x_copy(k, side):
            src, dst = ((0, nx), (nx - 1, -1))[side]
            return pltpu.make_async_remote_copy(
                B.at[k, slab(src)], B.at[k, slab(dst)], xs.at[k, side], xr.at[k, 1 - side],
                device_id={"gx": gx + 2 * side - 1}, device_id_type=MESH)

        def y_copy(k, side):
            return pltpu.make_async_remote_copy(
                YS.at[k, side], YG.at[k, 1 - side], ys.at[k, side], yr.at[k, 1 - side],
                device_id={"gy": gy + 2 * side - 1}, device_id_type=MESH)

        def z_copy(k, side):
            return pltpu.make_async_remote_copy(
                ZS.at[k], ZG.at[k, 1 - side], zs.at[k, side], zr.at[k, 1 - side],
                device_id={"gz": gz + 2 * side - 1}, device_id_type=MESH)

        copies = (x_copy, y_copy, z_copy)

        def on_sides(axes, act_on):
            for axis in axes:
                for side, there in ((0, low), (1, high)):
                    @pl.when(there[axis])
                    def _():
                        act_on(copies[axis], side)

        def send(k, axes):
            on_sides(axes, lambda copy, side: copy(k, side).start())

        def arrive(k, axes=(0, 1, 2)):
            on_sides(axes, lambda copy, side: copy(k, 1 - side).wait_recv())

        y_rows = tuple(pl.ds(row(0) + y, nx, stride=pitch) for y in (0, ny - 1))

        def y_pack(k):
            for side in range(2):
                YS[k, side] = B[k, y_rows[side], :]

        def packed(value, x, t):
            return turn(jnp.where(ends, value, 0.0), place(x, t)[1])

        def unpacked(value, x, t):
            half, amount = place(x, t)
            return jnp.where(ends, turn(value[half], -amount), 0.0)

        def z_ghost(k):
            return [jnp.where(odd, turn(ZG[k, 1, half], -1), turn(ZG[k, 0, half], 1))
                    for half in range(halves)]

        for part in range(nx // chunk):
            for copy in load_copies(part):
                copy.wait()
            sums = {}
            for x in range(part * chunk, (part + 1) * chunk):
                for t in range(tiles):
                    rows = pl.ds(8 * t, 8)
                    liquid = act_v[x, rows, :].astype(F32)
                    w, b = inv_v[x, rows, :] * liquid, rs_v[x, rows, :] * liquid
                    B[WEIGHT, at(x, t), :] = w
                    B[0, at(x, t), :] = b
                    half = place(x, t)[0]
                    for k, value in ((WEIGHT, w), (0, b)):
                        sums.setdefault((k, half), Sums()).add(packed(value, x, t))
            for (k, half), total in sums.items():
                begins = place(part * chunk, 0)[1] == 0
                ZS[k, half] = total.total() if begins else ZS[k, half] + total.total()
        y_pack(WEIGHT)
        y_pack(0)
        pl.semaphore_wait(barrier, present)
        send(WEIGHT, (0, 1, 2))
        send(0, (0, 1, 2))
        greet(far.at[0], chip_peer(1))
        greet(far.at[0], chip_peer(chips - 1))

        for x in range(nx):
            for t in range(tiles):
                w = B[WEIGHT, at(x, t), :]
                if x < nx - 1:
                    HX[flat(x + 1, t), :] = scaled_face(w, B[WEIGHT, at(x + 1, t), :])
                HY[at(x, t), :] = scaled_face(w, B[WEIGHT, near(row(x, t) - 1), :])
                upper = scaled_face(w, jnp.where(last, 0.0, turn(w, -1)))
                HZP[flat(x, t), :] = upper
                HZM[flat(x, t), :] = jnp.where(first, 0.0, turn(upper, 1))
            for t in range(tiles):
                w = B[WEIGHT, at(x, t), :]
                dry = w * (-1.0 / SHIFT)
                terms = []
                for inside, other, face in (
                    (x < nx - 1, lambda: B[WEIGHT, at(x + 1, t), :], lambda: HX[flat(x + 1, t), :]),
                    (x > 0, lambda: B[WEIGHT, at(x - 1, t), :], lambda: HX[flat(x, t), :]),
                    (True, lambda: B[WEIGHT, near(row(x, t) + 1), :], lambda: HY[near(row(x, t) + 1), :]),
                    (True, lambda: B[WEIGHT, near(row(x, t) - 1), :], lambda: HY[at(x, t), :]),
                    (True, lambda: jnp.where(last, 0.0, turn(w, -1)), lambda: HZP[flat(x, t), :]),
                    (True, lambda: jnp.where(first, 0.0, turn(w, 1)), lambda: HZM[flat(x, t), :]),
                ):
                    terms.append(jnp.where(other() > 0.0, face(), dry) if inside else dry)
                D[flat(x, t), :] = -1.0 - tree(terms)

        arrive(WEIGHT)

        def ghost_face(here, other):
            face = scaled_face(here, other)
            return face, jnp.where(other > 0.0, here * (-1.0 / SHIFT) - face, 0.0)

        for side, x, there in ((0, 0, -1), (1, nx - 1, nx)):
            for t in range(tiles):
                face, change = ghost_face(B[WEIGHT, at(x, t), :], B[WEIGHT, at(there, t), :])
                HX[flat((0, nx)[side], t), :] = face
                D[flat(x, t), :] = D[flat(x, t), :] + change
        for side in range(2):
            face, change = ghost_face(B[WEIGHT, y_rows[side], :], YG[WEIGHT, side])
            HYG[side] = face
            rows = pl.ds((0, ny - 1)[side], nx, stride=ny)
            D[rows, :] = D[rows, :] + change
        ghosts = z_ghost(WEIGHT)
        changes = []
        for half in range(halves):
            face, change = ghost_face(ZS[WEIGHT, half], ghosts[half])
            FP[half] = face
            changes.append(change)
        for x, t in every:
            D[flat(x, t), :] = D[flat(x, t), :] + unpacked(changes, x, t)

        def moments(k, before):
            mixed, square = Sums(), Sums()
            for x, t in every:
                value = B[k, at(x, t), :]
                mixed.add(value * B[before, at(x, t), :])
                square.add(value * value)
            MU[2 * k] = mixed.total()
            MU[2 * k + 1] = square.total()

        @pl.loop(0, STEPS)
        def _(k):
            before = jnp.maximum(k - 1, 0)
            mixed, square = Sums(), Sums()
            ahead = [Sums() for _ in range(halves)]
            for x, t in every:
                center = B[k, at(x, t), :]
                terms = [D[flat(x, t), :] * center]
                if x < nx - 1:
                    terms.append(HX[flat(x + 1, t), :] * B[k, at(x + 1, t), :])
                if x > 0:
                    terms.append(HX[flat(x, t), :] * B[k, at(x - 1, t), :])
                terms.append(HY[near(row(x, t) + 1), :] * B[k, near(row(x, t) + 1), :])
                terms.append(HY[at(x, t), :] * B[k, near(row(x, t) - 1), :])
                terms.append(HZP[flat(x, t), :] * turn(center, -1))
                terms.append(HZM[flat(x, t), :] * turn(center, 1))
                image = tree(terms)
                B[k + 1, at(x, t), :] = image
                mixed.add(center * B[before, at(x, t), :])
                square.add(center * center)
                if not is_rim(x, t):
                    ahead[place(x, t)[0]].add(packed(image, x, t))
            MU[2 * k] = mixed.total()
            MU[2 * k + 1] = square.total()
            for half in range(halves):
                ZS[k + 1, half] = ahead[half].total()

            for when, round_id in ((1, 0), (3, 1)):
                @pl.when(k == when)
                def _():
                    pl.semaphore_wait(far.at[round_id], 2)
                    greet(far.at[round_id + 1], chip_peer(2 << round_id))
                    greet(far.at[round_id + 1], chip_peer(chips - (2 << round_id)))

            arrive(k)
            for side in range(2):
                B[k + 1, y_rows[side], :] = B[k + 1, y_rows[side], :] + HYG[side] * YG[k, side]
            ghosts = z_ghost(k)
            extra = [FP[half] * ghosts[half] for half in range(halves)]
            rim = [Sums() for _ in range(halves)]
            for x, t in caps:
                face, there = (0, -1) if x == 0 else (nx, nx)
                value = B[k + 1, at(x, t), :] + HX[flat(face, t), :] * B[k, at(there, t), :]
                rim[place(x, t)[0]].add(packed(value, x, t))
                B[k + 1, at(x, t), :] = value + unpacked(extra, x, t)

            @pl.when(k < STEPS - 1)
            def _():
                send(k + 1, (0,))

            for x, t in sides_y:
                value = B[k + 1, at(x, t), :]
                rim[place(x, t)[0]].add(packed(value, x, t))
                B[k + 1, at(x, t), :] = value + unpacked(extra, x, t)
            for half in range(halves):
                ZS[k + 1, half] = ZS[k + 1, half] + (rim[half].total() + extra[half])

            @pl.when(k < STEPS - 1)
            def _():
                y_pack(k + 1)
                send(k + 1, (2, 1))

            for x, t in inner:
                B[k + 1, at(x, t), :] = B[k + 1, at(x, t), :] + unpacked(extra, x, t)

        moments(STEPS, STEPS - 1)

        local = jnp.sum(jnp.sum(MU[...], axis=1), axis=1, keepdims=True)
        diagonal = (lax.broadcasted_iota(jnp.int32, (16, LANES), 0)
                    == lax.broadcasted_iota(jnp.int32, (16, LANES), 1))
        line = jnp.sum(jnp.where(diagonal, jnp.broadcast_to(local, (16, LANES)), 0.0), axis=0, keepdims=True)

        def all_sum(line, staged, landed, sent, got, me, peers, meanwhile):
            staged[...] = line
            landed[me] = line
            for peer in peers:
                pltpu.make_async_remote_copy(
                    staged, landed.at[me], sent, got, device_id=peer, device_id_type=MESH).start()
            meanwhile()
            others = landed.at[pl.ds(0, len(peers))]
            pltpu.make_async_copy(others, others, got).wait()
            return tree([landed[i] for i in range(len(peers) + 1)])

        def drain_halos():
            for k in SLOTS:
                on_sides((0, 1, 2), lambda copy, side: copy(k, side).wait_send())

        def far_known():
            pl.semaphore_wait(far.at[2], 2)

        plane_peers = []
        for c in range(2):
            for dy in range(gyn):
                for dz in range(gzn):
                    if c or dy or dz:
                        plane_peers.append({
                            "gx": gx + 1 - 2 * core if c else gx,
                            "gy": (gy + dy) % gyn, "gz": (gz + dz) % gzn})
        line = all_sum(line, SA, RA, a_send, a_recv, core + 2 * (gy + gyn * gz), plane_peers, far_known)
        line = all_sum(line, SB, RB, b_send, b_recv, chip, [chip_peer(d) for d in range(1, chips)], drain_halos)

        spread = jnp.broadcast_to(line, (8, LANES))
        mu = [jnp.broadcast_to(spread[:, i + 1 : i + 2], (8, LANES)) for i in range(MOMENTS)]
        gram = [[mu[i + j] for j in range(SIZE)] for i in range(SIZE)]
        right = [jnp.full((8, LANES), (-1.0) ** i, F32) for i in range(SIZE)]
        inverse = []
        for p in range(SIZE):
            inverse.append(1.0 / gram[p][p])
            for i in range(p + 1, SIZE):
                factor = gram[p][i] * inverse[p]
                for j in range(i, SIZE):
                    gram[i][j] = gram[i][j] - factor * gram[p][j]
                right[i] = right[i] - factor * right[p]
        solved = [None] * SIZE
        for i in reversed(range(SIZE)):
            running = right[i]
            for j in reversed(range(i + 1, SIZE)):
                running = running - gram[i][j] * solved[j]
            solved[i] = running * inverse[i]
        norm = 1.0 / tree([value if i % 2 == 0 else -value for i, value in enumerate(solved)])
        leftover = [value * norm for value in solved]
        scaled = [None] * STEPS
        scaled[STEPS - 1] = -leftover[STEPS]
        for i in reversed(range(STEPS - 1)):
            scaled[i] = -leftover[i + 1] - scaled[i + 1]
        weights = [value * (1.0 / SHIFT) for value in scaled]

        def out_copies(part):
            where = pl.ds(part * chunk, chunk)
            return [pltpu.make_async_copy(src.at[where], dst.at[where], out_sem.at[i, part])
                    for i, (src, dst) in enumerate(((OS, sol), (OR, res)))]

        @pl.loop(0, nx // chunk)
        def _(part):
            for within in range(chunk):
                x = part * chunk + within
                for t in range(tiles):
                    where = pl.ds(pl.multiple_of((x + 1) * pitch + 8 + 8 * t, 8), 8)
                    values = [B[i, where, :] for i in range(SIZE)]
                    OS[x, pl.ds(8 * t, 8), :] = tree([weights[i] * values[i] for i in range(STEPS)])
                    OR[x, pl.ds(8 * t, 8), :] = tree([leftover[i] * values[i] for i in range(SIZE)])

            for copy in out_copies(part):
                copy.start()

        for landed, sent, count in ((RA, a_send, plane), (RB, b_send, chips)):
            others = landed.at[pl.ds(0, count - 1)]
            pltpu.make_async_copy(others, others, sent).wait()

        @pl.loop(0, nx // chunk)
        def _(part):
            for copy in out_copies(part):
                copy.wait()

    scratch = [
        pltpu.VMEM((nx, ny, nz), F32), pltpu.VMEM((nx, ny, nz), F32), pltpu.VMEM((nx, ny, nz), jnp.int32),
        pltpu.VMEM((8, (nx + 2) * pitch, LANES), F32),
        pltpu.VMEM((8, 2, nx, LANES), F32), pltpu.VMEM((8, 2, nx, LANES), F32),
        pltpu.VMEM((8, halves, 8, LANES), F32), pltpu.VMEM((8, 2, halves, 8, LANES), F32),
        pltpu.VMEM(((nx + 1) * ny, LANES), F32), pltpu.VMEM(((nx + 2) * pitch, LANES), F32),
        pltpu.VMEM((2, nx, LANES), F32),
        pltpu.VMEM((nx * ny, LANES), F32), pltpu.VMEM((nx * ny, LANES), F32),
        pltpu.VMEM((halves, 8, LANES), F32),
        pltpu.VMEM((nx * ny, LANES), F32),
        pltpu.VMEM((16, 8, LANES), F32),
        pltpu.VMEM((1, LANES), F32), pltpu.VMEM((plane, 1, LANES), F32),
        pltpu.VMEM((1, LANES), F32), pltpu.VMEM((chips, 1, LANES), F32),
        pltpu.VMEM((nx, ny, nz), F32), pltpu.VMEM((nx, ny, nz), F32),
        pltpu.SemaphoreType.DMA((3, nx // chunk)), pltpu.SemaphoreType.DMA((2, nx // chunk)),
    ] + [pltpu.SemaphoreType.DMA((8, 2))] * 6 + [pltpu.SemaphoreType.DMA] * 4 + [
        pltpu.SemaphoreType.REGULAR((3,))]
    return kernel, scratch


def solution(mesh):
    counts = tuple(mesh.shape[axis] for axis in ("gx", "gy", "gz"))

    def on_device(right_side, inv_density, active):
        kernel, scratch = make_kernel(right_side.shape, counts)
        field = jax.ShapeDtypeStruct(right_side.shape, F32)
        return pl.pallas_call(
            kernel,
            out_shape=(field, field),
            in_specs=[pl.BlockSpec(memory_space=pl.ANY)] * 3,
            out_specs=(pl.BlockSpec(memory_space=pl.ANY),) * 2,
            scratch_shapes=scratch,
            compiler_params=pltpu.CompilerParams(collective_id=0, has_side_effects=True),
        )(right_side, inv_density, active)

    placed = P("gx", "gy", "gz")
    return jax.shard_map(
        on_device, mesh=mesh, in_specs=(placed,) * 3, out_specs=(placed,) * 2, check_vma=False)
```

```python
import jax
import jax.numpy as jnp
from jax import lax
from jax.experimental import pallas as pl
from jax.experimental.pallas import tpu as pltpu
from jax.sharding import PartitionSpec as P

STEPS = 6
SIZE = STEPS + 1
MOMENTS = 2 * STEPS + 1
SHIFT = 7.0
MESH = pl.DeviceIdType.MESH
F32 = jnp.float32
LANES = 128
WEIGHT = 7
SLOTS = tuple(range(STEPS)) + (WEIGHT,)


def scaled_face(here, other):
    total = jnp.where(other > 0.0, here + other, 1.0)
    return (here * (-2.0 / SHIFT)) * other / total


def tree(values):
    values = list(values)
    while len(values) > 1:
        values = [values[i] + values[i + 1] if i + 1 < len(values) else values[i]
                  for i in range(0, len(values), 2)]
    return values[0]


class Sums:
    def __init__(self, count=4):
        self.parts, self.turn = [None] * count, 0

    def add(self, value):
        held = self.parts[self.turn]
        self.parts[self.turn] = value if held is None else held + value
        self.turn = (self.turn + 1) % len(self.parts)

    def total(self):
        return tree([part for part in self.parts if part is not None])


def make_kernel(shape, counts):
    nx, ny, nz = shape
    gxn, gyn, gzn = counts
    tiles = ny // 8
    pitch = ny + 16
    halves = nx * tiles * 2 // LANES
    plane = 2 * gyn * gzn
    chips = gxn // 2
    chunk = 4

    def row(x, t=0):
        return (x + 1) * pitch + 8 + 8 * t

    def at(x, t):
        return pl.ds(row(x, t), 8)

    def flat(x, t):
        return pl.ds(x * ny + 8 * t, 8)

    def slab(x):
        return pl.ds(row(x), ny)

    def place(x, t):
        j = x * tiles + t
        return j // (LANES // 2), 2 * (j % (LANES // 2))

    def turn(value, amount):
        amount %= LANES
        return pltpu.roll(value, amount, 1) if amount else value

    def is_rim(x, t):
        return x in (0, nx - 1) or t in (0, tiles - 1)

    every = [(x, t) for x in range(nx) for t in range(tiles)]
    inner = [xt for xt in every if not is_rim(*xt)]
    caps = [xt for xt in every if xt[0] in (0, nx - 1)]
    sides_y = [xt for xt in every if is_rim(*xt) and xt[0] not in (0, nx - 1)]

    def kernel(rs, inv, act, B, FACTORS, rs_v, inv_v, act_v, YS, YG, ZS, ZG,
               HX, HY, HYG, HZM, HZP, FP, CP, D, LS, SA, RA, SB, RB,
               in_sem, xs, xr, ys, yr, zs, zr, a_send, a_recv, b_send, b_recv, far):
        gx, gy, gz = lax.axis_index("gx"), lax.axis_index("gy"), lax.axis_index("gz")
        chip, core = gx // 2, gx % 2
        nil = gx // 4096

        def near(start):
            return pl.ds(nil + start, 8)

        def load_copies(part):
            where = pl.ds(part * chunk, chunk)
            return [pltpu.make_async_copy(src.at[where], dst.at[where], in_sem.at[i, part])
                    for i, (src, dst) in enumerate(((rs, rs_v), (inv, inv_v), (act, act_v)))]

        for part in range(nx // chunk):
            for copy in load_copies(part):
                copy.start()

        low = (gx > 0, gy > 0, gz > 0)
        high = (gx < gxn - 1, gy < gyn - 1, gz < gzn - 1)
        names = ("gx", "gy", "gz")
        pos = (gx, gy, gz)

        def chip_peer(d):
            return {"gx": (gx + 2 * d) % gxn}

        barrier = pltpu.get_barrier_semaphore()

        def greet(semaphore, device):
            pl.semaphore_signal(semaphore, inc=1, device_id=device, device_id_type=MESH)

        present = 2
        for axis in range(3):
            for there, step in ((low, -1), (high, 1)):
                present = present + there[axis].astype(jnp.int32)

                @pl.when(there[axis])
                def _():
                    greet(barrier, {names[axis]: pos[axis] + step})

        greet(barrier, chip_peer(1))
        greet(barrier, chip_peer(chips - 1))

        for side, there in ((0, low), (1, high)):
            @pl.when(jnp.logical_not(there[0]))
            def _():
                for k in SLOTS:
                    B[k, slab((-1, nx)[side]), :] = jnp.zeros((ny, LANES), F32)

            @pl.when(jnp.logical_not(there[1]))
            def _():
                for k in SLOTS:
                    YG[k, side] = jnp.zeros((nx, LANES), F32)

            @pl.when(jnp.logical_not(there[2]))
            def _():
                for k in SLOTS:
                    ZG[k, side] = jnp.zeros((halves, 8, LANES), F32)

        none = jnp.zeros((nx, LANES), F32)
        for k in SLOTS:
            B[k, pl.ds(row(0) - 1, nx, stride=pitch), :] = none
            B[k, pl.ds(row(0) + ny, nx, stride=pitch), :] = none
        HY[pl.ds(row(0) + ny, nx, stride=pitch), :] = none
        LS[...] = jnp.zeros((16, LANES), F32)

        lane = lax.broadcasted_iota(jnp.int32, (8, LANES), 1)
        first, last = lane == 0, lane == LANES - 1
        ends = first | last
        odd = lane % 2 == 1

        def x_copy(k, side):
            src, dst = ((0, nx), (nx - 1, -1))[side]
            return pltpu.make_async_remote_copy(
                B.at[k, slab(src)], B.at[k, slab(dst)], xs.at[k, side], xr.at[k, 1 - side],
                device_id={"gx": gx + 2 * side - 1}, device_id_type=MESH)

        def y_copy(k, side):
            return pltpu.make_async_remote_copy(
                YS.at[k, side], YG.at[k, 1 - side], ys.at[k, side], yr.at[k, 1 - side],
                device_id={"gy": gy + 2 * side - 1}, device_id_type=MESH)

        def z_copy(k, side):
            return pltpu.make_async_remote_copy(
                ZS.at[k], ZG.at[k, 1 - side], zs.at[k, side], zr.at[k, 1 - side],
                device_id={"gz": gz + 2 * side - 1}, device_id_type=MESH)

        copies = (x_copy, y_copy, z_copy)

        def on_sides(axes, act_on):
            for axis in axes:
                for side, there in ((0, low), (1, high)):
                    @pl.when(there[axis])
                    def _():
                        act_on(copies[axis], side)

        def send(k, axes):
            on_sides(axes, lambda copy, side: copy(k, side).start())

        def arrive(k, axes=(0, 1, 2)):
            on_sides(axes, lambda copy, side: copy(k, 1 - side).wait_recv())

        y_rows = tuple(pl.ds(row(0) + y, nx, stride=pitch) for y in (0, ny - 1))

        def y_pack(k):
            for side in range(2):
                YS[k, side] = B[k, y_rows[side], :]

        def packed(value, x, t):
            return turn(jnp.where(ends, value, 0.0), place(x, t)[1])

        def unpacked(value, x, t):
            half, amount = place(x, t)
            return jnp.where(ends, turn(value[half], -amount), 0.0)

        def z_ghost(k):
            return [jnp.where(odd, turn(ZG[k, 1, half], -1), turn(ZG[k, 0, half], 1))
                    for half in range(halves)]

        for part in range(nx // chunk):
            for copy in load_copies(part):
                copy.wait()
            sums = {}
            for x in range(part * chunk, (part + 1) * chunk):
                for t in range(tiles):
                    rows = pl.ds(8 * t, 8)
                    liquid = act_v[x, rows, :].astype(F32)
                    w, b = inv_v[x, rows, :] * liquid, rs_v[x, rows, :] * liquid
                    B[WEIGHT, at(x, t), :] = w
                    B[0, at(x, t), :] = b
                    half = place(x, t)[0]
                    for k, value in ((WEIGHT, w), (0, b)):
                        sums.setdefault((k, half), Sums()).add(packed(value, x, t))
            for (k, half), total in sums.items():
                begins = place(part * chunk, 0)[1] == 0
                ZS[k, half] = total.total() if begins else ZS[k, half] + total.total()
        y_pack(WEIGHT)
        y_pack(0)
        pl.semaphore_wait(barrier, present)
        send(WEIGHT, (0, 1, 2))
        send(0, (0, 1, 2))
        greet(far.at[0], chip_peer(1))
        greet(far.at[0], chip_peer(chips - 1))

        for x in range(nx):
            for t in range(tiles):
                w = B[WEIGHT, at(x, t), :]
                if x < nx - 1:
                    HX[flat(x + 1, t), :] = scaled_face(w, B[WEIGHT, at(x + 1, t), :])
                HY[at(x, t), :] = scaled_face(w, B[WEIGHT, near(row(x, t) - 1), :])
                upper = scaled_face(w, jnp.where(last, 0.0, turn(w, -1)))
                HZP[flat(x, t), :] = upper
                HZM[flat(x, t), :] = jnp.where(first, 0.0, turn(upper, 1))
            for t in range(tiles):
                w = B[WEIGHT, at(x, t), :]
                dry = w * (-1.0 / SHIFT)
                terms = []
                for inside, other, face in (
                    (x < nx - 1, lambda: B[WEIGHT, at(x + 1, t), :], lambda: HX[flat(x + 1, t), :]),
                    (x > 0, lambda: B[WEIGHT, at(x - 1, t), :], lambda: HX[flat(x, t), :]),
                    (True, lambda: B[WEIGHT, near(row(x, t) + 1), :], lambda: HY[near(row(x, t) + 1), :]),
                    (True, lambda: B[WEIGHT, near(row(x, t) - 1), :], lambda: HY[at(x, t), :]),
                    (True, lambda: jnp.where(last, 0.0, turn(w, -1)), lambda: HZP[flat(x, t), :]),
                    (True, lambda: jnp.where(first, 0.0, turn(w, 1)), lambda: HZM[flat(x, t), :]),
                ):
                    terms.append(jnp.where(other() > 0.0, face(), dry) if inside else dry)
                D[flat(x, t), :] = -1.0 - tree(terms)

        def ghost_face(here, other):
            face = scaled_face(here, other)
            return face, jnp.where(other > 0.0, here * (-1.0 / SHIFT) - face, 0.0)

        def ghost_faces():
            arrive(WEIGHT)
            for side, x, there in ((0, 0, -1), (1, nx - 1, nx)):
                for t in range(tiles):
                    face, change = ghost_face(B[WEIGHT, at(x, t), :], B[WEIGHT, at(there, t), :])
                    HX[flat((0, nx)[side], t), :] = face
                    D[flat(x, t), :] = D[flat(x, t), :] + change
                    B[1, at(x, t), :] = B[1, at(x, t), :] + change * B[0, at(x, t), :]
            for side in range(2):
                face, change = ghost_face(B[WEIGHT, y_rows[side], :], YG[WEIGHT, side])
                HYG[side] = face
                rows = pl.ds((0, ny - 1)[side], nx, stride=ny)
                D[rows, :] = D[rows, :] + change
                B[1, y_rows[side], :] = B[1, y_rows[side], :] + change * B[0, y_rows[side], :]
            ghosts = z_ghost(WEIGHT)
            for half in range(halves):
                FP[half], CP[half] = ghost_face(ZS[WEIGHT, half], ghosts[half])

        def settle_diagonal():
            changes = [CP[half] for half in range(halves)]
            for x, t in every:
                D[flat(x, t), :] = D[flat(x, t), :] + unpacked(changes, x, t)
            for half in range(halves):
                CP[half] = jnp.zeros((8, LANES), F32)

        def keep(k, mixed, square):
            for offset, value in enumerate((mixed, square)):
                LS[pl.ds(2 * k + offset, 1), :] = jnp.sum(value.total(), axis=0, keepdims=True)

        def moments(k, before):
            mixed, square = Sums(), Sums()
            for x, t in every:
                value = B[k, at(x, t), :]
                mixed.add(value * B[before, at(x, t), :])
                square.add(value * value)
            keep(k, mixed, square)

        @pl.loop(0, STEPS)
        def _(k):
            before = jnp.maximum(k - 1, 0)
            mixed, square = Sums(), Sums()
            ahead = [Sums() for _ in range(halves)]
            for x, t in every:
                center = B[k, at(x, t), :]
                terms = [D[flat(x, t), :] * center]
                if x < nx - 1:
                    terms.append(HX[flat(x + 1, t), :] * B[k, at(x + 1, t), :])
                if x > 0:
                    terms.append(HX[flat(x, t), :] * B[k, at(x - 1, t), :])
                terms.append(HY[near(row(x, t) + 1), :] * B[k, near(row(x, t) + 1), :])
                terms.append(HY[at(x, t), :] * B[k, near(row(x, t) - 1), :])
                terms.append(HZP[flat(x, t), :] * turn(center, -1))
                terms.append(HZM[flat(x, t), :] * turn(center, 1))
                image = tree(terms)
                B[k + 1, at(x, t), :] = image
                mixed.add(center * B[before, at(x, t), :])
                square.add(center * center)
                if not is_rim(x, t):
                    ahead[place(x, t)[0]].add(packed(image, x, t))
            keep(k, mixed, square)
            for half in range(halves):
                ZS[k + 1, half] = ahead[half].total()

            for when, round_id in ((1, 0), (3, 1)):
                @pl.when(k == when)
                def _():
                    pl.semaphore_wait(far.at[round_id], 2)
                    greet(far.at[round_id + 1], chip_peer(2 << round_id))
                    greet(far.at[round_id + 1], chip_peer(chips - (2 << round_id)))

            @pl.when(k == 0)
            def _():
                ghost_faces()

            arrive(k)
            for side in range(2):
                B[k + 1, y_rows[side], :] = B[k + 1, y_rows[side], :] + HYG[side] * YG[k, side]
            ghosts = z_ghost(k)
            extra = [FP[half] * ghosts[half] + CP[half] * ZS[k, half] for half in range(halves)]
            rim = [Sums() for _ in range(halves)]
            for x, t in caps:
                face, there = (0, -1) if x == 0 else (nx, nx)
                value = B[k + 1, at(x, t), :] + HX[flat(face, t), :] * B[k, at(there, t), :]
                rim[place(x, t)[0]].add(packed(value, x, t))
                B[k + 1, at(x, t), :] = value + unpacked(extra, x, t)

            @pl.when(k < STEPS - 1)
            def _():
                send(k + 1, (0,))

            for x, t in sides_y:
                value = B[k + 1, at(x, t), :]
                rim[place(x, t)[0]].add(packed(value, x, t))
                B[k + 1, at(x, t), :] = value + unpacked(extra, x, t)
            for half in range(halves):
                ZS[k + 1, half] = ZS[k + 1, half] + (rim[half].total() + extra[half])

            @pl.when(k < STEPS - 1)
            def _():
                y_pack(k + 1)
                send(k + 1, (2, 1))

            for x, t in inner:
                B[k + 1, at(x, t), :] = B[k + 1, at(x, t), :] + unpacked(extra, x, t)

            @pl.when(k == 0)
            def _():
                settle_diagonal()

        moments(STEPS, STEPS - 1)

        local = jnp.sum(LS[...], axis=1, keepdims=True)
        diagonal = (lax.broadcasted_iota(jnp.int32, (16, LANES), 0)
                    == lax.broadcasted_iota(jnp.int32, (16, LANES), 1))
        line = jnp.sum(jnp.where(diagonal, jnp.broadcast_to(local, (16, LANES)), 0.0), axis=0, keepdims=True)

        def all_sum(line, staged, landed, sent, got, me, peers, meanwhile):
            staged[...] = line
            landed[me] = line
            for peer in peers:
                pltpu.make_async_remote_copy(
                    staged, landed.at[me], sent, got, device_id=peer, device_id_type=MESH).start()
            meanwhile()
            others = landed.at[pl.ds(0, len(peers))]
            pltpu.make_async_copy(others, others, got).wait()
            return tree([landed[i] for i in range(len(peers) + 1)])

        def drain_halos():
            for k in SLOTS:
                on_sides((0, 1, 2), lambda copy, side: copy(k, side).wait_send())

        def far_known():
            pl.semaphore_wait(far.at[2], 2)

        def hops(count, d):
            return min(d, count - d)

        plane_peers = []
        for c in range(2):
            for dy in range(gyn):
                for dz in range(gzn):
                    if c or dy or dz:
                        plane_peers.append((hops(gyn, dy) + hops(gzn, dz), {
                            "gx": gx + 1 - 2 * core if c else gx,
                            "gy": (gy + dy) % gyn, "gz": (gz + dz) % gzn}))
        plane_peers = [peer for _, peer in sorted(plane_peers, key=lambda pair: -pair[0])]
        chip_steps = sorted(range(1, chips), key=lambda d: -hops(chips, d))
        line = all_sum(line, SA, RA, a_send, a_recv, core + 2 * (gy + gyn * gz), plane_peers, far_known)
        line = all_sum(line, SB, RB, b_send, b_recv, chip, [chip_peer(d) for d in chip_steps], drain_halos)

        spread = jnp.broadcast_to(line, (8, LANES))
        mu = [jnp.broadcast_to(spread[:, i + 1 : i + 2], (8, LANES)) for i in range(MOMENTS)]
        gram = [[mu[i + j] for j in range(SIZE)] for i in range(SIZE)]
        right = [jnp.full((8, LANES), (-1.0) ** i, F32) for i in range(SIZE)]
        inverse = []
        for p in range(SIZE):
            inverse.append(1.0 / gram[p][p])
            for i in range(p + 1, SIZE):
                factor = gram[p][i] * inverse[p]
                for j in range(i, SIZE):
                    gram[i][j] = gram[i][j] - factor * gram[p][j]
                right[i] = right[i] - factor * right[p]
        solved = [None] * SIZE
        for i in reversed(range(SIZE)):
            running = right[i]
            for j in reversed(range(i + 1, SIZE)):
                running = running - gram[i][j] * solved[j]
            solved[i] = running * inverse[i]
        norm = 1.0 / tree([value if i % 2 == 0 else -value for i, value in enumerate(solved)])
        leftover = [value * norm for value in solved]
        scaled = [None] * STEPS
        scaled[STEPS - 1] = -leftover[STEPS]
        for i in reversed(range(STEPS - 1)):
            scaled[i] = -leftover[i + 1] - scaled[i + 1]
        weights = [value * (1.0 / SHIFT) for value in scaled]

        for i, value in enumerate(weights + leftover):
            FACTORS[i] = value
        for landed, sent, count in ((RA, a_send, plane), (RB, b_send, chips)):
            others = landed.at[pl.ds(0, count - 1)]
            pltpu.make_async_copy(others, others, sent).wait()

    def combine(B, FACTORS, sol, res, OS, OR, out_sem):
        weights = [FACTORS[i] for i in range(STEPS)]
        leftover = [FACTORS[STEPS + i] for i in range(SIZE)]

        def out_copies(part):
            where = pl.ds(part * chunk, chunk)
            return [pltpu.make_async_copy(src.at[where], dst.at[where], out_sem.at[i, part])
                    for i, (src, dst) in enumerate(((OS, sol), (OR, res)))]

        @pl.loop(0, nx // chunk)
        def _(part):
            for within in range(chunk):
                x = part * chunk + within
                for t in range(tiles):
                    where = pl.ds(pl.multiple_of((x + 1) * pitch + 8 + 8 * t, 8), 8)
                    values = [B[i, where, :] for i in range(SIZE)]
                    OS[x, pl.ds(8 * t, 8), :] = tree([weights[i] * values[i] for i in range(STEPS)])
                    OR[x, pl.ds(8 * t, 8), :] = tree([leftover[i] * values[i] for i in range(SIZE)])

            for copy in out_copies(part):
                copy.start()

        @pl.loop(0, nx // chunk)
        def _(part):
            for copy in out_copies(part):
                copy.wait()

    results = (jax.ShapeDtypeStruct((8, (nx + 2) * pitch, LANES), F32),
               jax.ShapeDtypeStruct((MOMENTS, 8, LANES), F32))
    outs = [pltpu.VMEM((nx, ny, nz), F32), pltpu.VMEM((nx, ny, nz), F32),
            pltpu.SemaphoreType.DMA((2, nx // chunk))]
    scratch = [
        pltpu.VMEM((nx, ny, nz), F32), pltpu.VMEM((nx, ny, nz), F32), pltpu.VMEM((nx, ny, nz), jnp.int32),
        pltpu.VMEM((8, 2, nx, LANES), F32), pltpu.VMEM((8, 2, nx, LANES), F32),
        pltpu.VMEM((8, halves, 8, LANES), F32), pltpu.VMEM((8, 2, halves, 8, LANES), F32),
        pltpu.VMEM(((nx + 1) * ny, LANES), F32), pltpu.VMEM(((nx + 2) * pitch, LANES), F32),
        pltpu.VMEM((2, nx, LANES), F32),
        pltpu.VMEM((nx * ny, LANES), F32), pltpu.VMEM((nx * ny, LANES), F32),
        pltpu.VMEM((halves, 8, LANES), F32), pltpu.VMEM((halves, 8, LANES), F32),
        pltpu.VMEM((nx * ny, LANES), F32),
        pltpu.VMEM((16, LANES), F32),
        pltpu.VMEM((1, LANES), F32), pltpu.VMEM((plane, 1, LANES), F32),
        pltpu.VMEM((1, LANES), F32), pltpu.VMEM((chips, 1, LANES), F32),
        pltpu.SemaphoreType.DMA((3, nx // chunk)),
    ] + [pltpu.SemaphoreType.DMA((8, 2))] * 6 + [pltpu.SemaphoreType.DMA] * 4 + [
        pltpu.SemaphoreType.REGULAR((3,))]
    return kernel, results, scratch, combine, outs


def solution(mesh):
    counts = tuple(mesh.shape[axis] for axis in ("gx", "gy", "gz"))

    def on_device(right_side, inv_density, active):
        kernel, results, scratch, combine, outs = make_kernel(right_side.shape, counts)
        whole = pl.BlockSpec(memory_space=pltpu.VMEM)
        basis, factors = pl.pallas_call(
            kernel,
            out_shape=results,
            in_specs=[pl.BlockSpec(memory_space=pltpu.HBM)] * 3,
            out_specs=(whole, whole),
            scratch_shapes=scratch,
            compiler_params=pltpu.CompilerParams(
                collective_id=0, has_side_effects=True, vmem_limit_bytes=16 << 20),
        )(right_side, inv_density, active)
        field = jax.ShapeDtypeStruct(right_side.shape, F32)
        return pl.pallas_call(
            combine,
            out_shape=(field, field),
            in_specs=[whole, whole],
            out_specs=(pl.BlockSpec(memory_space=pltpu.HBM),) * 2,
            scratch_shapes=outs,
            compiler_params=pltpu.CompilerParams(vmem_limit_bytes=16 << 20),
        )(basis, factors)

    placed = P("gx", "gy", "gz")
    return jax.shard_map(
        on_device, mesh=mesh, in_specs=(placed,) * 3, out_specs=(placed,) * 2, check_vma=False)
```

```python
import jax
import jax.numpy as jnp
from jax import lax
from jax.experimental import pallas as pl
from jax.experimental.pallas import tpu as pltpu
from jax.sharding import PartitionSpec as P

STEPS = 6
SIZE = STEPS + 1
MOMENTS = 2 * STEPS + 1
SHIFT = 7.0
MESH = pl.DeviceIdType.MESH
F32 = jnp.float32
LANES = 128
WEIGHT = 7
SLOTS = tuple(range(STEPS)) + (WEIGHT,)


def scaled_face(here, other):
    total = jnp.where(other > 0.0, here + other, 1.0)
    return (here * (-2.0 / SHIFT)) * other / total


def tree(values):
    values = list(values)
    while len(values) > 1:
        values = [values[i] + values[i + 1] if i + 1 < len(values) else values[i]
                  for i in range(0, len(values), 2)]
    return values[0]


class Sums:
    def __init__(self, count=4):
        self.parts, self.turn = [None] * count, 0

    def add(self, value):
        held = self.parts[self.turn]
        self.parts[self.turn] = value if held is None else held + value
        self.turn = (self.turn + 1) % len(self.parts)

    def total(self):
        return tree([part for part in self.parts if part is not None])


def make_kernel(shape, counts):
    nx, ny, nz = shape
    gxn, gyn, gzn = counts
    tiles = ny // 8
    pitch = ny + 16
    halves = nx * tiles * 2 // LANES
    plane = 2 * gyn * gzn
    chips = gxn // 2
    chunk = 4

    def row(x, t=0):
        return (x + 1) * pitch + 8 + 8 * t

    def at(x, t):
        return pl.ds(row(x, t), 8)

    def flat(x, t):
        return pl.ds(x * ny + 8 * t, 8)

    def slab(x):
        return pl.ds(row(x), ny)

    def place(x, t):
        j = x * tiles + t
        return j // (LANES // 2), 2 * (j % (LANES // 2))

    def turn(value, amount):
        amount %= LANES
        return pltpu.roll(value, amount, 1) if amount else value

    def is_rim(x, t):
        return x in (0, nx - 1) or t in (0, tiles - 1)

    every = [(x, t) for x in range(nx) for t in range(tiles)]
    inner = [xt for xt in every if not is_rim(*xt)]
    caps = [xt for xt in every if xt[0] in (0, nx - 1)]
    sides_y = [xt for xt in every if is_rim(*xt) and xt[0] not in (0, nx - 1)]

    def kernel(rs, inv, act, B, FACTORS, rs_v, inv_v, act_v, YS, YG, ZS, ZG,
               HX, HY, HYG, HZM, HZP, FP, CP, D, LS, SA, RA, SB, RB,
               in_sem, xs, xr, ys, yr, zs, zr, a_send, a_recv, b_send, b_recv, far):
        gx, gy, gz = lax.axis_index("gx"), lax.axis_index("gy"), lax.axis_index("gz")
        chip, core = gx // 2, gx % 2
        nil = gx // 4096

        def near(start):
            return pl.ds(nil + start, 8)

        def load_copies(part):
            where = pl.ds(part * chunk, chunk)
            return [pltpu.make_async_copy(src.at[where], dst.at[where], in_sem.at[i, part])
                    for i, (src, dst) in enumerate(((rs, rs_v), (inv, inv_v), (act, act_v)))]

        for part in range(nx // chunk):
            for copy in load_copies(part):
                copy.start()

        low = (gx > 0, gy > 0, gz > 0)
        high = (gx < gxn - 1, gy < gyn - 1, gz < gzn - 1)
        names = ("gx", "gy", "gz")
        pos = (gx, gy, gz)

        def chip_peer(d):
            return {"gx": (gx + 2 * d) % gxn}

        barrier = pltpu.get_barrier_semaphore()

        def greet(semaphore, device):
            pl.semaphore_signal(semaphore, inc=1, device_id=device, device_id_type=MESH)

        present = 2
        for axis in range(3):
            for there, step in ((low, -1), (high, 1)):
                present = present + there[axis].astype(jnp.int32)

                @pl.when(there[axis])
                def _():
                    greet(barrier, {names[axis]: pos[axis] + step})

        greet(barrier, chip_peer(1))
        greet(barrier, chip_peer(chips - 1))

        for side, there in ((0, low), (1, high)):
            @pl.when(jnp.logical_not(there[0]))
            def _():
                for k in SLOTS:
                    B[k, slab((-1, nx)[side]), :] = jnp.zeros((ny, LANES), F32)

            @pl.when(jnp.logical_not(there[1]))
            def _():
                for k in SLOTS:
                    YG[k, side] = jnp.zeros((nx, LANES), F32)

            @pl.when(jnp.logical_not(there[2]))
            def _():
                for k in SLOTS:
                    ZG[k, side] = jnp.zeros((halves, 8, LANES), F32)

        none = jnp.zeros((nx, LANES), F32)
        for k in SLOTS:
            B[k, pl.ds(row(0) - 1, nx, stride=pitch), :] = none
            B[k, pl.ds(row(0) + ny, nx, stride=pitch), :] = none
        HY[pl.ds(row(0) + ny, nx, stride=pitch), :] = none
        LS[...] = jnp.zeros((16, LANES), F32)

        lane = lax.broadcasted_iota(jnp.int32, (8, LANES), 1)
        first, last = lane == 0, lane == LANES - 1
        ends = first | last
        odd = lane % 2 == 1

        def x_copy(k, side):
            src, dst = ((0, nx), (nx - 1, -1))[side]
            return pltpu.make_async_remote_copy(
                B.at[k, slab(src)], B.at[k, slab(dst)], xs.at[k, side], xr.at[k, 1 - side],
                device_id={"gx": gx + 2 * side - 1}, device_id_type=MESH)

        def y_copy(k, side):
            return pltpu.make_async_remote_copy(
                YS.at[k, side], YG.at[k, 1 - side], ys.at[k, side], yr.at[k, 1 - side],
                device_id={"gy": gy + 2 * side - 1}, device_id_type=MESH)

        def z_copy(k, side):
            return pltpu.make_async_remote_copy(
                ZS.at[k], ZG.at[k, 1 - side], zs.at[k, side], zr.at[k, 1 - side],
                device_id={"gz": gz + 2 * side - 1}, device_id_type=MESH)

        copies = (x_copy, y_copy, z_copy)

        def on_sides(axes, act_on):
            for axis in axes:
                for side, there in ((0, low), (1, high)):
                    @pl.when(there[axis])
                    def _():
                        act_on(copies[axis], side)

        def send(k, axes):
            on_sides(axes, lambda copy, side: copy(k, side).start())

        def arrive(k, axes=(0, 1, 2)):
            on_sides(axes, lambda copy, side: copy(k, 1 - side).wait_recv())

        y_rows = tuple(pl.ds(row(0) + y, nx, stride=pitch) for y in (0, ny - 1))

        def y_pack(k):
            for side in range(2):
                YS[k, side] = B[k, y_rows[side], :]

        def packed(value, x, t):
            return turn(jnp.where(ends, value, 0.0), place(x, t)[1])

        def unpacked(value, x, t):
            half, amount = place(x, t)
            return jnp.where(ends, turn(value[half], -amount), 0.0)

        def z_ghost(k):
            return [jnp.where(odd, turn(ZG[k, 1, half], -1), turn(ZG[k, 0, half], 1))
                    for half in range(halves)]

        for part in range(nx // chunk):
            for copy in load_copies(part):
                copy.wait()
            sums = {}
            for x in range(part * chunk, (part + 1) * chunk):
                for t in range(tiles):
                    rows = pl.ds(8 * t, 8)
                    liquid = act_v[x, rows, :].astype(F32)
                    w, b = inv_v[x, rows, :] * liquid, rs_v[x, rows, :] * liquid
                    B[WEIGHT, at(x, t), :] = w
                    B[0, at(x, t), :] = b
                    half = place(x, t)[0]
                    for k, value in ((WEIGHT, w), (0, b)):
                        sums.setdefault((k, half), Sums()).add(packed(value, x, t))
            for (k, half), total in sums.items():
                begins = place(part * chunk, 0)[1] == 0
                ZS[k, half] = total.total() if begins else ZS[k, half] + total.total()
        y_pack(WEIGHT)
        y_pack(0)
        pl.semaphore_wait(barrier, present)
        send(WEIGHT, (0, 1, 2))
        send(0, (0, 1, 2))
        greet(far.at[0], chip_peer(1))
        greet(far.at[0], chip_peer(chips - 1))

        for x in range(nx):
            for t in range(tiles):
                w = B[WEIGHT, at(x, t), :]
                if x < nx - 1:
                    HX[flat(x + 1, t), :] = scaled_face(w, B[WEIGHT, at(x + 1, t), :])
                HY[at(x, t), :] = scaled_face(w, B[WEIGHT, near(row(x, t) - 1), :])
                upper = scaled_face(w, jnp.where(last, 0.0, turn(w, -1)))
                HZP[flat(x, t), :] = upper
                HZM[flat(x, t), :] = jnp.where(first, 0.0, turn(upper, 1))
            for t in range(tiles):
                w = B[WEIGHT, at(x, t), :]
                dry = w * (-1.0 / SHIFT)
                terms = []
                for inside, other, face in (
                    (x < nx - 1, lambda: B[WEIGHT, at(x + 1, t), :], lambda: HX[flat(x + 1, t), :]),
                    (x > 0, lambda: B[WEIGHT, at(x - 1, t), :], lambda: HX[flat(x, t), :]),
                    (True, lambda: B[WEIGHT, near(row(x, t) + 1), :], lambda: HY[near(row(x, t) + 1), :]),
                    (True, lambda: B[WEIGHT, near(row(x, t) - 1), :], lambda: HY[at(x, t), :]),
                    (True, lambda: jnp.where(last, 0.0, turn(w, -1)), lambda: HZP[flat(x, t), :]),
                    (True, lambda: jnp.where(first, 0.0, turn(w, 1)), lambda: HZM[flat(x, t), :]),
                ):
                    terms.append(jnp.where(other() > 0.0, face(), dry) if inside else dry)
                D[flat(x, t), :] = -1.0 - tree(terms)

        def ghost_face(here, other):
            face = scaled_face(here, other)
            return face, jnp.where(other > 0.0, here * (-1.0 / SHIFT) - face, 0.0)

        def ghost_faces():
            arrive(WEIGHT)
            for side, x, there in ((0, 0, -1), (1, nx - 1, nx)):
                for t in range(tiles):
                    face, change = ghost_face(B[WEIGHT, at(x, t), :], B[WEIGHT, at(there, t), :])
                    HX[flat((0, nx)[side], t), :] = face
                    D[flat(x, t), :] = D[flat(x, t), :] + change
                    B[1, at(x, t), :] = B[1, at(x, t), :] + change * B[0, at(x, t), :]
            for side in range(2):
                face, change = ghost_face(B[WEIGHT, y_rows[side], :], YG[WEIGHT, side])
                HYG[side] = face
                rows = pl.ds((0, ny - 1)[side], nx, stride=ny)
                D[rows, :] = D[rows, :] + change
                B[1, y_rows[side], :] = B[1, y_rows[side], :] + change * B[0, y_rows[side], :]
            ghosts = z_ghost(WEIGHT)
            for half in range(halves):
                FP[half], CP[half] = ghost_face(ZS[WEIGHT, half], ghosts[half])

        def settle_diagonal():
            changes = [CP[half] for half in range(halves)]
            for x, t in every:
                D[flat(x, t), :] = D[flat(x, t), :] + unpacked(changes, x, t)
            for half in range(halves):
                CP[half] = jnp.zeros((8, LANES), F32)

        def keep(k, mixed, square):
            for offset, value in enumerate((mixed, square)):
                LS[pl.ds(2 * k + offset, 1), :] = jnp.sum(value.total(), axis=0, keepdims=True)

        def moments(k, before):
            mixed, square = Sums(), Sums()
            for x, t in every:
                value = B[k, at(x, t), :]
                mixed.add(value * B[before, at(x, t), :])
                square.add(value * value)
            keep(k, mixed, square)

        @pl.loop(0, STEPS)
        def _(k):
            before = jnp.maximum(k - 1, 0)
            mixed, square = Sums(), Sums()
            ahead = [Sums() for _ in range(halves)]
            for x, t in every:
                center = B[k, at(x, t), :]
                terms = [D[flat(x, t), :] * center]
                if x < nx - 1:
                    terms.append(HX[flat(x + 1, t), :] * B[k, at(x + 1, t), :])
                if x > 0:
                    terms.append(HX[flat(x, t), :] * B[k, at(x - 1, t), :])
                terms.append(HY[near(row(x, t) + 1), :] * B[k, near(row(x, t) + 1), :])
                terms.append(HY[at(x, t), :] * B[k, near(row(x, t) - 1), :])
                terms.append(HZP[flat(x, t), :] * turn(center, -1))
                terms.append(HZM[flat(x, t), :] * turn(center, 1))
                image = tree(terms)
                B[k + 1, at(x, t), :] = image
                mixed.add(center * B[before, at(x, t), :])
                square.add(center * center)
                if not is_rim(x, t):
                    ahead[place(x, t)[0]].add(packed(image, x, t))
            keep(k, mixed, square)
            for half in range(halves):
                ZS[k + 1, half] = ahead[half].total()

            for when, round_id in ((1, 0), (3, 1)):
                @pl.when(k == when)
                def _():
                    pl.semaphore_wait(far.at[round_id], 2)
                    greet(far.at[round_id + 1], chip_peer(2 << round_id))
                    greet(far.at[round_id + 1], chip_peer(chips - (2 << round_id)))

            @pl.when(k == 0)
            def _():
                ghost_faces()

            arrive(k)
            for side in range(2):
                B[k + 1, y_rows[side], :] = B[k + 1, y_rows[side], :] + HYG[side] * YG[k, side]
            ghosts = z_ghost(k)
            extra = [FP[half] * ghosts[half] + CP[half] * ZS[k, half] for half in range(halves)]
            rim = [Sums() for _ in range(halves)]
            for x, t in caps:
                face, there = (0, -1) if x == 0 else (nx, nx)
                value = B[k + 1, at(x, t), :] + HX[flat(face, t), :] * B[k, at(there, t), :]
                rim[place(x, t)[0]].add(packed(value, x, t))
                B[k + 1, at(x, t), :] = value + unpacked(extra, x, t)

            @pl.when(k < STEPS - 1)
            def _():
                send(k + 1, (0,))

            for x, t in sides_y:
                value = B[k + 1, at(x, t), :]
                rim[place(x, t)[0]].add(packed(value, x, t))
                B[k + 1, at(x, t), :] = value + unpacked(extra, x, t)
            for half in range(halves):
                ZS[k + 1, half] = ZS[k + 1, half] + (rim[half].total() + extra[half])

            @pl.when(k < STEPS - 1)
            def _():
                y_pack(k + 1)
                send(k + 1, (2, 1))

            for x, t in inner:
                B[k + 1, at(x, t), :] = B[k + 1, at(x, t), :] + unpacked(extra, x, t)

            @pl.when(k == 0)
            def _():
                settle_diagonal()

        moments(STEPS, STEPS - 1)

        local = jnp.sum(LS[...], axis=1, keepdims=True)
        diagonal = (lax.broadcasted_iota(jnp.int32, (16, LANES), 0)
                    == lax.broadcasted_iota(jnp.int32, (16, LANES), 1))
        line = jnp.sum(jnp.where(diagonal, jnp.broadcast_to(local, (16, LANES)), 0.0), axis=0, keepdims=True)

        def all_sum(line, staged, landed, sent, got, me, peers, meanwhile):
            staged[...] = line
            landed[me] = line
            for peer in peers:
                pltpu.make_async_remote_copy(
                    staged, landed.at[me], sent, got, device_id=peer, device_id_type=MESH).start()
            meanwhile()
            others = landed.at[pl.ds(0, len(peers))]
            pltpu.make_async_copy(others, others, got).wait()
            return tree([landed[i] for i in range(len(peers) + 1)])

        def drain_halos():
            for k in SLOTS:
                on_sides((0, 1, 2), lambda copy, side: copy(k, side).wait_send())

        def far_known():
            pl.semaphore_wait(far.at[2], 2)

        def hops(count, d):
            return min(d, count - d)

        plane_peers = []
        for c in range(2):
            for dy in range(gyn):
                for dz in range(gzn):
                    if c or dy or dz:
                        plane_peers.append((hops(gyn, dy) + hops(gzn, dz), {
                            "gx": gx + 1 - 2 * core if c else gx,
                            "gy": (gy + dy) % gyn, "gz": (gz + dz) % gzn}))
        plane_peers = [peer for _, peer in sorted(plane_peers, key=lambda pair: -pair[0])]
        chip_steps = sorted(range(1, chips), key=lambda d: -hops(chips, d))
        line = all_sum(line, SA, RA, a_send, a_recv, core + 2 * (gy + gyn * gz), plane_peers, far_known)
        line = all_sum(line, SB, RB, b_send, b_recv, chip, [chip_peer(d) for d in chip_steps], drain_halos)

        spread = jnp.broadcast_to(line, (8, LANES))
        mu = [jnp.broadcast_to(spread[:, i + 1 : i + 2], (8, LANES)) for i in range(MOMENTS)]
        gram = [[mu[i + j] for j in range(SIZE)] for i in range(SIZE)]
        right = [jnp.full((8, LANES), (-1.0) ** i, F32) for i in range(SIZE)]
        inverse = []
        for p in range(SIZE):
            inverse.append(1.0 / gram[p][p])
            for i in range(p + 1, SIZE):
                factor = gram[p][i] * inverse[p]
                for j in range(i, SIZE):
                    gram[i][j] = gram[i][j] - factor * gram[p][j]
                right[i] = right[i] - factor * right[p]
        solved = [None] * SIZE
        for i in reversed(range(SIZE)):
            running = right[i]
            for j in reversed(range(i + 1, SIZE)):
                running = running - gram[i][j] * solved[j]
            solved[i] = running * inverse[i]
        norm = 1.0 / tree([value if i % 2 == 0 else -value for i, value in enumerate(solved)])
        leftover = [value * norm for value in solved]
        scaled = [None] * STEPS
        scaled[STEPS - 1] = -leftover[STEPS]
        for i in reversed(range(STEPS - 1)):
            scaled[i] = -leftover[i + 1] - scaled[i + 1]
        weights = [value * (1.0 / SHIFT) for value in scaled]

        for i, value in enumerate(weights + leftover):
            FACTORS[i] = value
        for landed, sent, count in ((RA, a_send, plane), (RB, b_send, chips)):
            others = landed.at[pl.ds(0, count - 1)]
            pltpu.make_async_copy(others, others, sent).wait()

    def combine(B, FACTORS, sol, res, OS, OR, out_sem):
        weights = [FACTORS[i] for i in range(STEPS)]
        leftover = [FACTORS[STEPS + i] for i in range(SIZE)]

        def out_copies(part):
            where = pl.ds(part * chunk, chunk)
            return [pltpu.make_async_copy(src.at[where], dst.at[where], out_sem.at[i, part])
                    for i, (src, dst) in enumerate(((OS, sol), (OR, res)))]

        @pl.loop(0, nx // chunk)
        def _(part):
            for within in range(chunk):
                x = part * chunk + within
                for t in range(tiles):
                    where = pl.ds(pl.multiple_of((x + 1) * pitch + 8 + 8 * t, 8), 8)
                    values = [B[i, where, :] for i in range(SIZE)]
                    OS[x, pl.ds(8 * t, 8), :] = tree([weights[i] * values[i] for i in range(STEPS)])
                    OR[x, pl.ds(8 * t, 8), :] = tree([leftover[i] * values[i] for i in range(SIZE)])

            for copy in out_copies(part):
                copy.start()

        @pl.loop(0, nx // chunk)
        def _(part):
            for copy in out_copies(part):
                copy.wait()

    results = (jax.ShapeDtypeStruct((8, (nx + 2) * pitch, LANES), F32),
               jax.ShapeDtypeStruct((MOMENTS, 8, LANES), F32))
    outs = [pltpu.VMEM((nx, ny, nz), F32), pltpu.VMEM((nx, ny, nz), F32),
            pltpu.SemaphoreType.DMA((2, nx // chunk))]
    scratch = [
        pltpu.VMEM((nx, ny, nz), F32), pltpu.VMEM((nx, ny, nz), F32), pltpu.VMEM((nx, ny, nz), jnp.int32),
        pltpu.VMEM((8, 2, nx, LANES), F32), pltpu.VMEM((8, 2, nx, LANES), F32),
        pltpu.VMEM((8, halves, 8, LANES), F32), pltpu.VMEM((8, 2, halves, 8, LANES), F32),
        pltpu.VMEM(((nx + 1) * ny, LANES), F32), pltpu.VMEM(((nx + 2) * pitch, LANES), F32),
        pltpu.VMEM((2, nx, LANES), F32),
        pltpu.VMEM((nx * ny, LANES), F32), pltpu.VMEM((nx * ny, LANES), F32),
        pltpu.VMEM((halves, 8, LANES), F32), pltpu.VMEM((halves, 8, LANES), F32),
        pltpu.VMEM((nx * ny, LANES), F32),
        pltpu.VMEM((16, LANES), F32),
        pltpu.VMEM((1, LANES), F32), pltpu.VMEM((plane, 1, LANES), F32),
        pltpu.VMEM((1, LANES), F32), pltpu.VMEM((chips, 1, LANES), F32),
        pltpu.SemaphoreType.DMA((3, nx // chunk)),
    ] + [pltpu.SemaphoreType.DMA((8, 2))] * 6 + [pltpu.SemaphoreType.DMA] * 4 + [
        pltpu.SemaphoreType.REGULAR((3,))]
    return kernel, results, scratch, combine, outs


def solution(mesh):
    counts = tuple(mesh.shape[axis] for axis in ("gx", "gy", "gz"))

    def on_device(right_side, inv_density, active):
        kernel, results, scratch, combine, outs = make_kernel(right_side.shape, counts)
        whole = pl.BlockSpec(memory_space=pltpu.VMEM)
        basis, factors = pl.pallas_call(
            kernel,
            out_shape=results,
            in_specs=[pl.BlockSpec(memory_space=pltpu.HBM)] * 3,
            out_specs=(whole, whole),
            scratch_shapes=scratch,
            compiler_params=pltpu.CompilerParams(
                collective_id=0, has_side_effects=True, vmem_limit_bytes=16 << 20),
        )(*[pltpu.with_memory_space_constraint(a, pltpu.HBM) for a in (right_side, inv_density, active)])
        field = jax.ShapeDtypeStruct(right_side.shape, F32)
        return pl.pallas_call(
            combine,
            out_shape=(field, field),
            in_specs=[whole, whole],
            out_specs=(pl.BlockSpec(memory_space=pltpu.HBM),) * 2,
            scratch_shapes=outs,
            compiler_params=pltpu.CompilerParams(vmem_limit_bytes=16 << 20),
        )(basis, factors)

    placed = P("gx", "gy", "gz")
    return jax.shard_map(
        on_device, mesh=mesh, in_specs=(placed,) * 3, out_specs=(placed,) * 2, check_vma=False)
```

```python
import jax
import jax.numpy as jnp
from jax import lax
from jax.experimental import pallas as pl
from jax.experimental.pallas import tpu as pltpu
from jax.sharding import PartitionSpec as P

STEPS = 6
SIZE = STEPS + 1
MOMENTS = 2 * STEPS + 1
SHIFT = 7.0
MESH = pl.DeviceIdType.MESH
F32 = jnp.float32
LANES = 128
WEIGHT = 7
SLOTS = tuple(range(STEPS)) + (WEIGHT,)


def scaled_face(here, other):
    total = jnp.where(other > 0.0, here + other, 1.0)
    return (here * (-2.0 / SHIFT)) * other / total


def tree(values):
    values = list(values)
    while len(values) > 1:
        values = [values[i] + values[i + 1] if i + 1 < len(values) else values[i]
                  for i in range(0, len(values), 2)]
    return values[0]


class Sums:
    def __init__(self, count=4):
        self.parts, self.turn = [None] * count, 0

    def add(self, value):
        held = self.parts[self.turn]
        self.parts[self.turn] = value if held is None else held + value
        self.turn = (self.turn + 1) % len(self.parts)

    def total(self):
        return tree([part for part in self.parts if part is not None])


def make_kernel(shape, counts):
    nx, ny, nz = shape
    gxn, gyn, gzn = counts
    tiles = ny // 8
    pitch = ny + 16
    halves = nx * tiles * 2 // LANES
    plane = 2 * gyn * gzn
    chips = gxn // 2
    chunk = 4

    def row(x, t=0):
        return (x + 1) * pitch + 8 + 8 * t

    def at(x, t):
        return pl.ds(row(x, t), 8)

    def flat(x, t):
        return pl.ds(x * ny + 8 * t, 8)

    def slab(x):
        return pl.ds(row(x), ny)

    def place(x, t):
        j = x * tiles + t
        return j // (LANES // 2), 2 * (j % (LANES // 2))

    def turn(value, amount):
        amount %= LANES
        return pltpu.roll(value, amount, 1) if amount else value

    def is_rim(x, t):
        return x in (0, nx - 1) or t in (0, tiles - 1)

    every = [(x, t) for x in range(nx) for t in range(tiles)]
    inner = [xt for xt in every if not is_rim(*xt)]
    caps = [xt for xt in every if xt[0] in (0, nx - 1)]
    sides_y = [xt for xt in every if is_rim(*xt) and xt[0] not in (0, nx - 1)]

    def kernel(rs, inv, act, B, FACTORS, rs_v, inv_v, act_v, YS, YG, ZS, ZG,
               HX, HY, HYG, HZM, HZP, FP, CP, D, LS, SA, RA, SB, RB,
               in_sem, xs, xr, ys, yr, zs, zr, a_send, a_recv, b_send, b_recv, far):
        gx, gy, gz = lax.axis_index("gx"), lax.axis_index("gy"), lax.axis_index("gz")
        chip, core = gx // 2, gx % 2
        nil = gx // 4096

        def near(start):
            return pl.ds(nil + start, 8)

        def load_copies(part):
            where = pl.ds(part * chunk, chunk)
            return [pltpu.make_async_copy(src.at[where], dst.at[where], in_sem.at[i, part])
                    for i, (src, dst) in enumerate(((rs, rs_v), (inv, inv_v), (act, act_v)))]

        for part in range(nx // chunk):
            for copy in load_copies(part):
                copy.start()

        low = (gx > 0, gy > 0, gz > 0)
        high = (gx < gxn - 1, gy < gyn - 1, gz < gzn - 1)
        names = ("gx", "gy", "gz")
        pos = (gx, gy, gz)

        def chip_peer(d):
            return {"gx": (gx + 2 * d) % gxn}

        barrier = pltpu.get_barrier_semaphore()

        def greet(semaphore, device):
            pl.semaphore_signal(semaphore, inc=1, device_id=device, device_id_type=MESH)

        present = 2
        for axis in range(3):
            for there, step in ((low, -1), (high, 1)):
                present = present + there[axis].astype(jnp.int32)

                @pl.when(there[axis])
                def _():
                    greet(barrier, {names[axis]: pos[axis] + step})

        greet(barrier, chip_peer(1))
        greet(barrier, chip_peer(chips - 1))

        for side, there in ((0, low), (1, high)):
            @pl.when(jnp.logical_not(there[0]))
            def _():
                for k in SLOTS:
                    B[k, slab((-1, nx)[side]), :] = jnp.zeros((ny, LANES), F32)

            @pl.when(jnp.logical_not(there[1]))
            def _():
                for k in SLOTS:
                    YG[k, side] = jnp.zeros((nx, LANES), F32)

            @pl.when(jnp.logical_not(there[2]))
            def _():
                for k in SLOTS:
                    ZG[k, side] = jnp.zeros((halves, 8, LANES), F32)

        none = jnp.zeros((nx, LANES), F32)
        for k in SLOTS:
            B[k, pl.ds(row(0) - 1, nx, stride=pitch), :] = none
            B[k, pl.ds(row(0) + ny, nx, stride=pitch), :] = none
        HY[pl.ds(row(0) + ny, nx, stride=pitch), :] = none
        LS[...] = jnp.zeros((16, LANES), F32)

        lane = lax.broadcasted_iota(jnp.int32, (8, LANES), 1)
        first, last = lane == 0, lane == LANES - 1
        ends = first | last
        odd = lane % 2 == 1
        middle = []
        for half in range(halves):
            index = half * (LANES // 2) + ((lane + 1) % LANES) // 2
            x_at, t_at = index // tiles, index % tiles
            middle.append((x_at > 0) & (x_at < nx - 1) & (t_at > 0) & (t_at < tiles - 1))

        def x_copy(k, side):
            src, dst = ((0, nx), (nx - 1, -1))[side]
            return pltpu.make_async_remote_copy(
                B.at[k, slab(src)], B.at[k, slab(dst)], xs.at[k, side], xr.at[k, 1 - side],
                device_id={"gx": gx + 2 * side - 1}, device_id_type=MESH)

        def y_copy(k, side):
            return pltpu.make_async_remote_copy(
                YS.at[k, side], YG.at[k, 1 - side], ys.at[k, side], yr.at[k, 1 - side],
                device_id={"gy": gy + 2 * side - 1}, device_id_type=MESH)

        def z_copy(k, side):
            return pltpu.make_async_remote_copy(
                ZS.at[k], ZG.at[k, 1 - side], zs.at[k, side], zr.at[k, 1 - side],
                device_id={"gz": gz + 2 * side - 1}, device_id_type=MESH)

        copies = (x_copy, y_copy, z_copy)

        def on_sides(axes, act_on):
            for axis in axes:
                for side, there in ((0, low), (1, high)):
                    @pl.when(there[axis])
                    def _():
                        act_on(copies[axis], side)

        def send(k, axes):
            on_sides(axes, lambda copy, side: copy(k, side).start())

        def arrive(k, axes=(0, 1, 2)):
            on_sides(axes, lambda copy, side: copy(k, 1 - side).wait_recv())

        y_rows = tuple(pl.ds(row(0) + y, nx, stride=pitch) for y in (0, ny - 1))

        def y_pack(k):
            for side in range(2):
                YS[k, side] = B[k, y_rows[side], :]

        def packed(value, x, t):
            return turn(jnp.where(ends, value, 0.0), place(x, t)[1])

        def unpacked(value, x, t):
            half, amount = place(x, t)
            return jnp.where(ends, turn(value[half], -amount), 0.0)

        def z_ghost(k):
            return [jnp.where(odd, turn(ZG[k, 1, half], -1), turn(ZG[k, 0, half], 1))
                    for half in range(halves)]

        for part in range(nx // chunk):
            for copy in load_copies(part):
                copy.wait()
            sums = {}
            for x in range(part * chunk, (part + 1) * chunk):
                for t in range(tiles):
                    rows = pl.ds(8 * t, 8)
                    liquid = act_v[x, rows, :].astype(F32)
                    w, b = inv_v[x, rows, :] * liquid, rs_v[x, rows, :] * liquid
                    B[WEIGHT, at(x, t), :] = w
                    B[0, at(x, t), :] = b
                    half = place(x, t)[0]
                    for k, value in ((WEIGHT, w), (0, b)):
                        sums.setdefault((k, half), Sums()).add(packed(value, x, t))
            for (k, half), total in sums.items():
                begins = place(part * chunk, 0)[1] == 0
                ZS[k, half] = total.total() if begins else ZS[k, half] + total.total()
        y_pack(WEIGHT)
        y_pack(0)
        pl.semaphore_wait(barrier, present)
        send(WEIGHT, (0, 1, 2))
        send(0, (0, 1, 2))
        greet(far.at[0], chip_peer(1))
        greet(far.at[0], chip_peer(chips - 1))

        for x in range(nx):
            for t in range(tiles):
                w = B[WEIGHT, at(x, t), :]
                if x < nx - 1:
                    HX[flat(x + 1, t), :] = scaled_face(w, B[WEIGHT, at(x + 1, t), :])
                HY[at(x, t), :] = scaled_face(w, B[WEIGHT, near(row(x, t) - 1), :])
                upper = scaled_face(w, jnp.where(last, 0.0, turn(w, -1)))
                HZP[flat(x, t), :] = upper
                HZM[flat(x, t), :] = jnp.where(first, 0.0, turn(upper, 1))
            for t in range(tiles):
                w = B[WEIGHT, at(x, t), :]
                dry = w * (-1.0 / SHIFT)
                terms = []
                for inside, other, face in (
                    (x < nx - 1, lambda: B[WEIGHT, at(x + 1, t), :], lambda: HX[flat(x + 1, t), :]),
                    (x > 0, lambda: B[WEIGHT, at(x - 1, t), :], lambda: HX[flat(x, t), :]),
                    (True, lambda: B[WEIGHT, near(row(x, t) + 1), :], lambda: HY[near(row(x, t) + 1), :]),
                    (True, lambda: B[WEIGHT, near(row(x, t) - 1), :], lambda: HY[at(x, t), :]),
                    (True, lambda: jnp.where(last, 0.0, turn(w, -1)), lambda: HZP[flat(x, t), :]),
                    (True, lambda: jnp.where(first, 0.0, turn(w, 1)), lambda: HZM[flat(x, t), :]),
                ):
                    terms.append(jnp.where(other() > 0.0, face(), dry) if inside else dry)
                D[flat(x, t), :] = -1.0 - tree(terms)

        def ghost_face(here, other):
            face = scaled_face(here, other)
            return face, jnp.where(other > 0.0, here * (-1.0 / SHIFT) - face, 0.0)

        def ghost_faces():
            arrive(WEIGHT)
            for side, x, there in ((0, 0, -1), (1, nx - 1, nx)):
                for t in range(tiles):
                    face, change = ghost_face(B[WEIGHT, at(x, t), :], B[WEIGHT, at(there, t), :])
                    HX[flat((0, nx)[side], t), :] = face
                    D[flat(x, t), :] = D[flat(x, t), :] + change
                    B[1, at(x, t), :] = B[1, at(x, t), :] + change * B[0, at(x, t), :]
            for side in range(2):
                face, change = ghost_face(B[WEIGHT, y_rows[side], :], YG[WEIGHT, side])
                HYG[side] = face
                rows = pl.ds((0, ny - 1)[side], nx, stride=ny)
                D[rows, :] = D[rows, :] + change
                B[1, y_rows[side], :] = B[1, y_rows[side], :] + change * B[0, y_rows[side], :]
            ghosts = z_ghost(WEIGHT)
            for half in range(halves):
                FP[half], CP[half] = ghost_face(ZS[WEIGHT, half], ghosts[half])

        def settle_diagonal():
            changes = [CP[half] for half in range(halves)]
            for x, t in every:
                D[flat(x, t), :] = D[flat(x, t), :] + unpacked(changes, x, t)
            for half in range(halves):
                CP[half] = jnp.zeros((8, LANES), F32)

        def keep(k, mixed, square):
            for offset, value in enumerate((mixed, square)):
                LS[pl.ds(2 * k + offset, 1), :] = jnp.sum(value.total(), axis=0, keepdims=True)

        def moments(k, before):
            mixed, square = Sums(), Sums()
            for x, t in every:
                value = B[k, at(x, t), :]
                mixed.add(value * B[before, at(x, t), :])
                square.add(value * value)
            keep(k, mixed, square)

        @pl.loop(0, STEPS)
        def _(k):
            before = jnp.maximum(k - 1, 0)
            mixed, square = Sums(), Sums()
            ahead = [Sums() for _ in range(halves)]
            for x, t in every:
                center = B[k, at(x, t), :]
                terms = [D[flat(x, t), :] * center]
                if x < nx - 1:
                    terms.append(HX[flat(x + 1, t), :] * B[k, at(x + 1, t), :])
                if x > 0:
                    terms.append(HX[flat(x, t), :] * B[k, at(x - 1, t), :])
                terms.append(HY[near(row(x, t) + 1), :] * B[k, near(row(x, t) + 1), :])
                terms.append(HY[at(x, t), :] * B[k, near(row(x, t) - 1), :])
                terms.append(HZP[flat(x, t), :] * turn(center, -1))
                terms.append(HZM[flat(x, t), :] * turn(center, 1))
                image = tree(terms)
                B[k + 1, at(x, t), :] = image
                mixed.add(center * B[before, at(x, t), :])
                square.add(center * center)
                if not is_rim(x, t):
                    ahead[place(x, t)[0]].add(packed(image, x, t))
            keep(k, mixed, square)
            for half in range(halves):
                ZS[k + 1, half] = ahead[half].total()

            for when, round_id in ((1, 0), (3, 1)):
                @pl.when(k == when)
                def _():
                    pl.semaphore_wait(far.at[round_id], 2)
                    greet(far.at[round_id + 1], chip_peer(2 << round_id))
                    greet(far.at[round_id + 1], chip_peer(chips - (2 << round_id)))

            @pl.when(k == 0)
            def _():
                ghost_faces()

            arrive(k, (1, 2))
            for side in range(2):
                B[k + 1, y_rows[side], :] = B[k + 1, y_rows[side], :] + HYG[side] * YG[k, side]
            ghosts = z_ghost(k)
            extra = [FP[half] * ghosts[half] + CP[half] * ZS[k, half] for half in range(halves)]
            for x, t in caps:
                B[k + 1, at(x, t), :] = B[k + 1, at(x, t), :] + unpacked(extra, x, t)
            rim = [Sums() for _ in range(halves)]
            for x, t in sides_y:
                value = B[k + 1, at(x, t), :] + unpacked(extra, x, t)
                B[k + 1, at(x, t), :] = value
                rim[place(x, t)[0]].add(packed(value, x, t))
            for half in range(halves):
                ZS[k + 1, half] = ZS[k + 1, half] + (rim[half].total() + jnp.where(middle[half], extra[half], 0.0))

            arrive(k, (0,))
            cap = [Sums() for _ in range(halves)]
            for x, t in caps:
                face, there = (0, -1) if x == 0 else (nx, nx)
                value = B[k + 1, at(x, t), :] + HX[flat(face, t), :] * B[k, at(there, t), :]
                B[k + 1, at(x, t), :] = value
                cap[place(x, t)[0]].add(packed(value, x, t))

            @pl.when(k < STEPS - 1)
            def _():
                send(k + 1, (0,))

            for half in range(halves):
                ZS[k + 1, half] = ZS[k + 1, half] + cap[half].total()

            @pl.when(k < STEPS - 1)
            def _():
                y_pack(k + 1)
                send(k + 1, (2, 1))

            for x, t in inner:
                B[k + 1, at(x, t), :] = B[k + 1, at(x, t), :] + unpacked(extra, x, t)

            @pl.when(k == 0)
            def _():
                settle_diagonal()

        moments(STEPS, STEPS - 1)

        local = jnp.sum(LS[...], axis=1, keepdims=True)
        diagonal = (lax.broadcasted_iota(jnp.int32, (16, LANES), 0)
                    == lax.broadcasted_iota(jnp.int32, (16, LANES), 1))
        line = jnp.sum(jnp.where(diagonal, jnp.broadcast_to(local, (16, LANES)), 0.0), axis=0, keepdims=True)

        def all_sum(line, staged, landed, sent, got, me, peers, meanwhile):
            staged[...] = line
            landed[me] = line
            for peer in peers:
                pltpu.make_async_remote_copy(
                    staged, landed.at[me], sent, got, device_id=peer, device_id_type=MESH).start()
            meanwhile()
            others = landed.at[pl.ds(0, len(peers))]
            pltpu.make_async_copy(others, others, got).wait()
            return tree([landed[i] for i in range(len(peers) + 1)])

        def drain_halos():
            for k in SLOTS:
                on_sides((0, 1, 2), lambda copy, side: copy(k, side).wait_send())

        def far_known():
            pl.semaphore_wait(far.at[2], 2)

        def hops(count, d):
            return min(d, count - d)

        plane_peers = []
        for c in range(2):
            for dy in range(gyn):
                for dz in range(gzn):
                    if c or dy or dz:
                        plane_peers.append((hops(gyn, dy) + hops(gzn, dz), {
                            "gx": gx + 1 - 2 * core if c else gx,
                            "gy": (gy + dy) % gyn, "gz": (gz + dz) % gzn}))
        plane_peers = [peer for _, peer in sorted(plane_peers, key=lambda pair: -pair[0])]
        chip_steps = sorted(range(1, chips), key=lambda d: -hops(chips, d))
        line = all_sum(line, SA, RA, a_send, a_recv, core + 2 * (gy + gyn * gz), plane_peers, far_known)
        line = all_sum(line, SB, RB, b_send, b_recv, chip, [chip_peer(d) for d in chip_steps], drain_halos)

        spread = jnp.broadcast_to(line, (8, LANES))
        mu = [jnp.broadcast_to(spread[:, i + 1 : i + 2], (8, LANES)) for i in range(MOMENTS)]
        gram = [[mu[i + j] for j in range(SIZE)] for i in range(SIZE)]
        right = [jnp.full((8, LANES), (-1.0) ** i, F32) for i in range(SIZE)]
        inverse = []
        for p in range(SIZE):
            inverse.append(1.0 / gram[p][p])
            for i in range(p + 1, SIZE):
                factor = gram[p][i] * inverse[p]
                for j in range(i, SIZE):
                    gram[i][j] = gram[i][j] - factor * gram[p][j]
                right[i] = right[i] - factor * right[p]
        solved = [None] * SIZE
        for i in reversed(range(SIZE)):
            running = right[i]
            for j in reversed(range(i + 1, SIZE)):
                running = running - gram[i][j] * solved[j]
            solved[i] = running * inverse[i]
        norm = 1.0 / tree([value if i % 2 == 0 else -value for i, value in enumerate(solved)])
        leftover = [value * norm for value in solved]
        scaled = [None] * STEPS
        scaled[STEPS - 1] = -leftover[STEPS]
        for i in reversed(range(STEPS - 1)):
            scaled[i] = -leftover[i + 1] - scaled[i + 1]
        weights = [value * (1.0 / SHIFT) for value in scaled]

        for i, value in enumerate(weights + leftover):
            FACTORS[i] = value
        for landed, sent, count in ((RA, a_send, plane), (RB, b_send, chips)):
            others = landed.at[pl.ds(0, count - 1)]
            pltpu.make_async_copy(others, others, sent).wait()

    def combine(B, FACTORS, sol, res, OS, OR, out_sem):
        weights = [FACTORS[i] for i in range(STEPS)]
        leftover = [FACTORS[STEPS + i] for i in range(SIZE)]

        def out_copies(part):
            where = pl.ds(part * chunk, chunk)
            return [pltpu.make_async_copy(src.at[where], dst.at[where], out_sem.at[i, part])
                    for i, (src, dst) in enumerate(((OS, sol), (OR, res)))]

        @pl.loop(0, nx // chunk)
        def _(part):
            for within in range(chunk):
                x = part * chunk + within
                for t in range(tiles):
                    where = pl.ds(pl.multiple_of((x + 1) * pitch + 8 + 8 * t, 8), 8)
                    values = [B[i, where, :] for i in range(SIZE)]
                    OS[x, pl.ds(8 * t, 8), :] = tree([weights[i] * values[i] for i in range(STEPS)])
                    OR[x, pl.ds(8 * t, 8), :] = tree([leftover[i] * values[i] for i in range(SIZE)])

            for copy in out_copies(part):
                copy.start()

        @pl.loop(0, nx // chunk)
        def _(part):
            for copy in out_copies(part):
                copy.wait()

    results = (jax.ShapeDtypeStruct((8, (nx + 2) * pitch, LANES), F32),
               jax.ShapeDtypeStruct((MOMENTS, 8, LANES), F32))
    outs = [pltpu.VMEM((nx, ny, nz), F32), pltpu.VMEM((nx, ny, nz), F32),
            pltpu.SemaphoreType.DMA((2, nx // chunk))]
    scratch = [
        pltpu.VMEM((nx, ny, nz), F32), pltpu.VMEM((nx, ny, nz), F32), pltpu.VMEM((nx, ny, nz), jnp.int32),
        pltpu.VMEM((8, 2, nx, LANES), F32), pltpu.VMEM((8, 2, nx, LANES), F32),
        pltpu.VMEM((8, halves, 8, LANES), F32), pltpu.VMEM((8, 2, halves, 8, LANES), F32),
        pltpu.VMEM(((nx + 1) * ny, LANES), F32), pltpu.VMEM(((nx + 2) * pitch, LANES), F32),
        pltpu.VMEM((2, nx, LANES), F32),
        pltpu.VMEM((nx * ny, LANES), F32), pltpu.VMEM((nx * ny, LANES), F32),
        pltpu.VMEM((halves, 8, LANES), F32), pltpu.VMEM((halves, 8, LANES), F32),
        pltpu.VMEM((nx * ny, LANES), F32),
        pltpu.VMEM((16, LANES), F32),
        pltpu.VMEM((1, LANES), F32), pltpu.VMEM((plane, 1, LANES), F32),
        pltpu.VMEM((1, LANES), F32), pltpu.VMEM((chips, 1, LANES), F32),
        pltpu.SemaphoreType.DMA((3, nx // chunk)),
    ] + [pltpu.SemaphoreType.DMA((8, 2))] * 6 + [pltpu.SemaphoreType.DMA] * 4 + [
        pltpu.SemaphoreType.REGULAR((3,))]
    return kernel, results, scratch, combine, outs


def solution(mesh):
    counts = tuple(mesh.shape[axis] for axis in ("gx", "gy", "gz"))

    def on_device(right_side, inv_density, active):
        kernel, results, scratch, combine, outs = make_kernel(right_side.shape, counts)
        whole = pl.BlockSpec(memory_space=pltpu.VMEM)
        basis, factors = pl.pallas_call(
            kernel,
            out_shape=results,
            in_specs=[pl.BlockSpec(memory_space=pltpu.HBM)] * 3,
            out_specs=(whole, whole),
            scratch_shapes=scratch,
            compiler_params=pltpu.CompilerParams(
                collective_id=0, has_side_effects=True, vmem_limit_bytes=16 << 20),
        )(*[pltpu.with_memory_space_constraint(a, pltpu.HBM) for a in (right_side, inv_density, active)])
        field = jax.ShapeDtypeStruct(right_side.shape, F32)
        return pl.pallas_call(
            combine,
            out_shape=(field, field),
            in_specs=[whole, whole],
            out_specs=(pl.BlockSpec(memory_space=pltpu.HBM),) * 2,
            scratch_shapes=outs,
            compiler_params=pltpu.CompilerParams(vmem_limit_bytes=16 << 20),
        )(basis, factors)

    placed = P("gx", "gy", "gz")
    return jax.shard_map(
        on_device, mesh=mesh, in_specs=(placed,) * 3, out_specs=(placed,) * 2, check_vma=False)
```

```python
import jax
import jax.numpy as jnp
from jax import lax
from jax.experimental import pallas as pl
from jax.experimental.pallas import tpu as pltpu
from jax.sharding import PartitionSpec as P

STEPS = 6
SIZE = STEPS + 1
MOMENTS = 2 * STEPS + 1
SHIFT = 7.0
MESH = pl.DeviceIdType.MESH
F32 = jnp.float32
LANES = 128
WEIGHT = 7
SLOTS = tuple(range(STEPS)) + (WEIGHT,)


def scaled_face(here, other):
    total = jnp.where(other > 0.0, here + other, 1.0)
    return (here * (-2.0 / SHIFT)) * other / total


def tree(values):
    values = list(values)
    while len(values) > 1:
        values = [values[i] + values[i + 1] if i + 1 < len(values) else values[i]
                  for i in range(0, len(values), 2)]
    return values[0]


class Sums:
    def __init__(self, count=4):
        self.parts, self.turn = [None] * count, 0

    def add(self, value):
        held = self.parts[self.turn]
        self.parts[self.turn] = value if held is None else held + value
        self.turn = (self.turn + 1) % len(self.parts)

    def total(self):
        return tree([part for part in self.parts if part is not None])


def make_kernel(shape, counts):
    nx, ny, nz = shape
    gxn, gyn, gzn = counts
    tiles = ny // 8
    pitch = ny + 16
    halves = nx * tiles * 2 // LANES
    plane = 2 * gyn * gzn
    chips = gxn // 2
    chunk = 4

    def row(x, t=0):
        return (x + 1) * pitch + 8 + 8 * t

    def at(x, t):
        return pl.ds(row(x, t), 8)

    def flat(x, t):
        return pl.ds(x * ny + 8 * t, 8)

    def slab(x):
        return pl.ds(row(x), ny)

    def place(x, t):
        j = x * tiles + t
        return j // (LANES // 2), 2 * (j % (LANES // 2))

    def turn(value, amount):
        amount %= LANES
        return pltpu.roll(value, amount, 1) if amount else value

    def is_rim(x, t):
        return x in (0, nx - 1) or t in (0, tiles - 1)

    every = [(x, t) for x in range(nx) for t in range(tiles)]
    inner = [xt for xt in every if not is_rim(*xt)]
    caps = [xt for xt in every if xt[0] in (0, nx - 1)]
    sides_y = [xt for xt in every if is_rim(*xt) and xt[0] not in (0, nx - 1)]

    def kernel(rs, inv, act, B, FACTORS, rs_v, inv_v, act_v, YS, YG, ZS, ZG,
               HX, HY, HYG, HZM, HZP, FP, CP, D, LS, SA, RA, SB, RB,
               in_sem, xs, xr, ys, yr, zs, zr, a_send, a_recv, b_send, b_recv, far):
        gx, gy, gz = lax.axis_index("gx"), lax.axis_index("gy"), lax.axis_index("gz")
        chip, core = gx // 2, gx % 2
        nil = gx // 4096

        def near(start):
            return pl.ds(nil + start, 8)

        def load_copies(part):
            where = pl.ds(part * chunk, chunk)
            return [pltpu.make_async_copy(src.at[where], dst.at[where], in_sem.at[i, part])
                    for i, (src, dst) in enumerate(((rs, rs_v), (inv, inv_v), (act, act_v)))]

        low = (gx > 0, gy > 0, gz > 0)
        high = (gx < gxn - 1, gy < gyn - 1, gz < gzn - 1)
        names = ("gx", "gy", "gz")
        pos = (gx, gy, gz)

        def chip_peer(d):
            return {"gx": (gx + 2 * d) % gxn}

        barrier = pltpu.get_barrier_semaphore()

        def greet(semaphore, device):
            pl.semaphore_signal(semaphore, inc=1, device_id=device, device_id_type=MESH)

        present = 2
        for axis in range(3):
            for there, step in ((low, -1), (high, 1)):
                present = present + there[axis].astype(jnp.int32)

                @pl.when(there[axis])
                def _():
                    greet(barrier, {names[axis]: pos[axis] + step})

        greet(barrier, chip_peer(1))
        greet(barrier, chip_peer(chips - 1))

        outside = (0, nx // chunk - 1)
        order = outside + tuple(part for part in range(nx // chunk) if part not in outside)
        for part in order:
            for copy in load_copies(part):
                copy.start()

        for side, there in ((0, low), (1, high)):
            @pl.when(jnp.logical_not(there[0]))
            def _():
                for k in SLOTS:
                    B[k, slab((-1, nx)[side]), :] = jnp.zeros((ny, LANES), F32)

            @pl.when(jnp.logical_not(there[1]))
            def _():
                for k in SLOTS:
                    YG[k, side] = jnp.zeros((nx, LANES), F32)

            @pl.when(jnp.logical_not(there[2]))
            def _():
                for k in SLOTS:
                    ZG[k, side] = jnp.zeros((halves, 8, LANES), F32)

        none = jnp.zeros((nx, LANES), F32)
        for k in SLOTS:
            B[k, pl.ds(row(0) - 1, nx, stride=pitch), :] = none
            B[k, pl.ds(row(0) + ny, nx, stride=pitch), :] = none
        HY[pl.ds(row(0) + ny, nx, stride=pitch), :] = none
        LS[...] = jnp.zeros((16, LANES), F32)

        lane = lax.broadcasted_iota(jnp.int32, (8, LANES), 1)
        first, last = lane == 0, lane == LANES - 1
        ends = first | last
        odd = lane % 2 == 1
        middle = []
        for half in range(halves):
            index = half * (LANES // 2) + ((lane + 1) % LANES) // 2
            x_at, t_at = index // tiles, index % tiles
            middle.append((x_at > 0) & (x_at < nx - 1) & (t_at > 0) & (t_at < tiles - 1))

        def x_copy(k, side):
            src, dst = ((0, nx), (nx - 1, -1))[side]
            return pltpu.make_async_remote_copy(
                B.at[k, slab(src)], B.at[k, slab(dst)], xs.at[k, side], xr.at[k, 1 - side],
                device_id={"gx": gx + 2 * side - 1}, device_id_type=MESH)

        def y_copy(k, side):
            return pltpu.make_async_remote_copy(
                YS.at[k, side], YG.at[k, 1 - side], ys.at[k, side], yr.at[k, 1 - side],
                device_id={"gy": gy + 2 * side - 1}, device_id_type=MESH)

        def z_copy(k, side):
            return pltpu.make_async_remote_copy(
                ZS.at[k], ZG.at[k, 1 - side], zs.at[k, side], zr.at[k, 1 - side],
                device_id={"gz": gz + 2 * side - 1}, device_id_type=MESH)

        copies = (x_copy, y_copy, z_copy)

        def on_sides(axes, act_on):
            for axis in axes:
                for side, there in ((0, low), (1, high)):
                    @pl.when(there[axis])
                    def _():
                        act_on(copies[axis], side)

        def send(k, axes):
            on_sides(axes, lambda copy, side: copy(k, side).start())

        def arrive(k, axes=(0, 1, 2)):
            on_sides(axes, lambda copy, side: copy(k, 1 - side).wait_recv())

        y_rows = tuple(pl.ds(row(0) + y, nx, stride=pitch) for y in (0, ny - 1))

        def y_pack(k):
            for side in range(2):
                YS[k, side] = B[k, y_rows[side], :]

        def packed(value, x, t):
            return turn(jnp.where(ends, value, 0.0), place(x, t)[1])

        def unpacked(value, x, t):
            half, amount = place(x, t)
            return jnp.where(ends, turn(value[half], -amount), 0.0)

        def z_ghost(k):
            return [jnp.where(odd, turn(ZG[k, 1, half], -1), turn(ZG[k, 0, half], 1))
                    for half in range(halves)]

        sums = {}
        for part in order:
            for copy in load_copies(part):
                copy.wait()
            for x in range(part * chunk, (part + 1) * chunk):
                for t in range(tiles):
                    rows = pl.ds(8 * t, 8)
                    liquid = act_v[x, rows, :].astype(F32)
                    w, b = inv_v[x, rows, :] * liquid, rs_v[x, rows, :] * liquid
                    B[WEIGHT, at(x, t), :] = w
                    B[0, at(x, t), :] = b
                    half = place(x, t)[0]
                    for k, value in ((WEIGHT, w), (0, b)):
                        sums.setdefault((k, half), Sums(2)).add(packed(value, x, t))
            if part == outside[-1]:
                pl.semaphore_wait(barrier, present)
                send(WEIGHT, (0,))
                send(0, (0,))
        for (k, half), total in sums.items():
            ZS[k, half] = total.total()
        y_pack(WEIGHT)
        y_pack(0)
        send(WEIGHT, (2, 1))
        send(0, (2, 1))
        greet(far.at[0], chip_peer(1))
        greet(far.at[0], chip_peer(chips - 1))

        for x in range(nx):
            for t in range(tiles):
                w = B[WEIGHT, at(x, t), :]
                if x < nx - 1:
                    HX[flat(x + 1, t), :] = scaled_face(w, B[WEIGHT, at(x + 1, t), :])
                HY[at(x, t), :] = scaled_face(w, B[WEIGHT, near(row(x, t) - 1), :])
                upper = scaled_face(w, jnp.where(last, 0.0, turn(w, -1)))
                HZP[flat(x, t), :] = upper
                HZM[flat(x, t), :] = jnp.where(first, 0.0, turn(upper, 1))
            for t in range(tiles):
                w = B[WEIGHT, at(x, t), :]
                dry = w * (-1.0 / SHIFT)
                terms = []
                for inside, other, face in (
                    (x < nx - 1, lambda: B[WEIGHT, at(x + 1, t), :], lambda: HX[flat(x + 1, t), :]),
                    (x > 0, lambda: B[WEIGHT, at(x - 1, t), :], lambda: HX[flat(x, t), :]),
                    (True, lambda: B[WEIGHT, near(row(x, t) + 1), :], lambda: HY[near(row(x, t) + 1), :]),
                    (True, lambda: B[WEIGHT, near(row(x, t) - 1), :], lambda: HY[at(x, t), :]),
                    (True, lambda: jnp.where(last, 0.0, turn(w, -1)), lambda: HZP[flat(x, t), :]),
                    (True, lambda: jnp.where(first, 0.0, turn(w, 1)), lambda: HZM[flat(x, t), :]),
                ):
                    terms.append(jnp.where(other() > 0.0, face(), dry) if inside else dry)
                D[flat(x, t), :] = -1.0 - tree(terms)

        def ghost_face(here, other):
            face = scaled_face(here, other)
            return face, jnp.where(other > 0.0, here * (-1.0 / SHIFT) - face, 0.0)

        def ghost_faces():
            arrive(WEIGHT)
            for side, x, there in ((0, 0, -1), (1, nx - 1, nx)):
                for t in range(tiles):
                    face, change = ghost_face(B[WEIGHT, at(x, t), :], B[WEIGHT, at(there, t), :])
                    HX[flat((0, nx)[side], t), :] = face
                    D[flat(x, t), :] = D[flat(x, t), :] + change
                    B[1, at(x, t), :] = B[1, at(x, t), :] + change * B[0, at(x, t), :]
            for side in range(2):
                face, change = ghost_face(B[WEIGHT, y_rows[side], :], YG[WEIGHT, side])
                HYG[side] = face
                rows = pl.ds((0, ny - 1)[side], nx, stride=ny)
                D[rows, :] = D[rows, :] + change
                B[1, y_rows[side], :] = B[1, y_rows[side], :] + change * B[0, y_rows[side], :]
            ghosts = z_ghost(WEIGHT)
            for half in range(halves):
                FP[half], CP[half] = ghost_face(ZS[WEIGHT, half], ghosts[half])

        def settle_diagonal():
            changes = [CP[half] for half in range(halves)]
            for x, t in every:
                D[flat(x, t), :] = D[flat(x, t), :] + unpacked(changes, x, t)
            for half in range(halves):
                CP[half] = jnp.zeros((8, LANES), F32)

        def keep(k, mixed, square):
            for offset, value in enumerate((mixed, square)):
                LS[pl.ds(2 * k + offset, 1), :] = jnp.sum(value.total(), axis=0, keepdims=True)

        def moments(k, before):
            mixed, square = Sums(), Sums()
            for x, t in every:
                value = B[k, at(x, t), :]
                mixed.add(value * B[before, at(x, t), :])
                square.add(value * value)
            keep(k, mixed, square)

        @pl.loop(0, STEPS)
        def _(k):
            before = jnp.maximum(k - 1, 0)
            mixed, square = Sums(), Sums()
            ahead = [Sums() for _ in range(halves)]
            for x, t in every:
                center = B[k, at(x, t), :]
                terms = [D[flat(x, t), :] * center]
                if x < nx - 1:
                    terms.append(HX[flat(x + 1, t), :] * B[k, at(x + 1, t), :])
                if x > 0:
                    terms.append(HX[flat(x, t), :] * B[k, at(x - 1, t), :])
                terms.append(HY[near(row(x, t) + 1), :] * B[k, near(row(x, t) + 1), :])
                terms.append(HY[at(x, t), :] * B[k, near(row(x, t) - 1), :])
                terms.append(HZP[flat(x, t), :] * turn(center, -1))
                terms.append(HZM[flat(x, t), :] * turn(center, 1))
                image = tree(terms)
                B[k + 1, at(x, t), :] = image
                mixed.add(center * B[before, at(x, t), :])
                square.add(center * center)
                if not is_rim(x, t):
                    ahead[place(x, t)[0]].add(packed(image, x, t))
            keep(k, mixed, square)
            for half in range(halves):
                ZS[k + 1, half] = ahead[half].total()

            for when, round_id in ((1, 0), (3, 1)):
                @pl.when(k == when)
                def _():
                    pl.semaphore_wait(far.at[round_id], 2)
                    greet(far.at[round_id + 1], chip_peer(2 << round_id))
                    greet(far.at[round_id + 1], chip_peer(chips - (2 << round_id)))

            @pl.when(k == 0)
            def _():
                ghost_faces()

            arrive(k, (1, 2))
            for side in range(2):
                B[k + 1, y_rows[side], :] = B[k + 1, y_rows[side], :] + HYG[side] * YG[k, side]
            ghosts = z_ghost(k)
            extra = [FP[half] * ghosts[half] + CP[half] * ZS[k, half] for half in range(halves)]
            for x, t in caps:
                B[k + 1, at(x, t), :] = B[k + 1, at(x, t), :] + unpacked(extra, x, t)
            rim = [Sums() for _ in range(halves)]
            for x, t in sides_y:
                value = B[k + 1, at(x, t), :] + unpacked(extra, x, t)
                B[k + 1, at(x, t), :] = value
                rim[place(x, t)[0]].add(packed(value, x, t))
            for half in range(halves):
                ZS[k + 1, half] = ZS[k + 1, half] + (rim[half].total() + jnp.where(middle[half], extra[half], 0.0))

            arrive(k, (0,))
            cap = [Sums() for _ in range(halves)]
            for x, t in caps:
                face, there = (0, -1) if x == 0 else (nx, nx)
                value = B[k + 1, at(x, t), :] + HX[flat(face, t), :] * B[k, at(there, t), :]
                B[k + 1, at(x, t), :] = value
                cap[place(x, t)[0]].add(packed(value, x, t))

            @pl.when(k < STEPS - 1)
            def _():
                send(k + 1, (0,))

            for half in range(halves):
                ZS[k + 1, half] = ZS[k + 1, half] + cap[half].total()

            @pl.when(k < STEPS - 1)
            def _():
                y_pack(k + 1)
                send(k + 1, (2, 1))

            for x, t in inner:
                B[k + 1, at(x, t), :] = B[k + 1, at(x, t), :] + unpacked(extra, x, t)

            @pl.when(k == 0)
            def _():
                settle_diagonal()

        moments(STEPS, STEPS - 1)

        local = jnp.sum(LS[...], axis=1, keepdims=True)
        diagonal = (lax.broadcasted_iota(jnp.int32, (16, LANES), 0)
                    == lax.broadcasted_iota(jnp.int32, (16, LANES), 1))
        line = jnp.sum(jnp.where(diagonal, jnp.broadcast_to(local, (16, LANES)), 0.0), axis=0, keepdims=True)

        def all_sum(line, staged, landed, sent, got, me, peers, meanwhile):
            staged[...] = line
            landed[me] = line
            for peer in peers:
                pltpu.make_async_remote_copy(
                    staged, landed.at[me], sent, got, device_id=peer, device_id_type=MESH).start()
            meanwhile()
            others = landed.at[pl.ds(0, len(peers))]
            pltpu.make_async_copy(others, others, got).wait()
            return tree([landed[i] for i in range(len(peers) + 1)])

        def drain_halos():
            for k in SLOTS:
                on_sides((0, 1, 2), lambda copy, side: copy(k, side).wait_send())

        def far_known():
            pl.semaphore_wait(far.at[2], 2)

        def hops(count, d):
            return min(d, count - d)

        plane_peers = []
        for c in range(2):
            for dy in range(gyn):
                for dz in range(gzn):
                    if c or dy or dz:
                        plane_peers.append((hops(gyn, dy) + hops(gzn, dz), {
                            "gx": gx + 1 - 2 * core if c else gx,
                            "gy": (gy + dy) % gyn, "gz": (gz + dz) % gzn}))
        plane_peers = [peer for _, peer in sorted(plane_peers, key=lambda pair: -pair[0])]
        chip_steps = sorted(range(1, chips), key=lambda d: -hops(chips, d))
        line = all_sum(line, SA, RA, a_send, a_recv, core + 2 * (gy + gyn * gz), plane_peers, far_known)
        line = all_sum(line, SB, RB, b_send, b_recv, chip, [chip_peer(d) for d in chip_steps], drain_halos)

        spread = jnp.broadcast_to(line, (8, LANES))
        mu = [jnp.broadcast_to(spread[:, i + 1 : i + 2], (8, LANES)) for i in range(MOMENTS)]
        gram = [[mu[i + j] for j in range(SIZE)] for i in range(SIZE)]
        right = [jnp.full((8, LANES), (-1.0) ** i, F32) for i in range(SIZE)]
        inverse = []
        for p in range(SIZE):
            inverse.append(1.0 / gram[p][p])
            for i in range(p + 1, SIZE):
                factor = gram[p][i] * inverse[p]
                for j in range(i, SIZE):
                    gram[i][j] = gram[i][j] - factor * gram[p][j]
                right[i] = right[i] - factor * right[p]
        solved = [None] * SIZE
        for i in reversed(range(SIZE)):
            running = right[i]
            for j in reversed(range(i + 1, SIZE)):
                running = running - gram[i][j] * solved[j]
            solved[i] = running * inverse[i]
        norm = 1.0 / tree([value if i % 2 == 0 else -value for i, value in enumerate(solved)])
        leftover = [value * norm for value in solved]
        scaled = [None] * STEPS
        scaled[STEPS - 1] = -leftover[STEPS]
        for i in reversed(range(STEPS - 1)):
            scaled[i] = -leftover[i + 1] - scaled[i + 1]
        weights = [value * (1.0 / SHIFT) for value in scaled]

        for i, value in enumerate(weights + leftover):
            FACTORS[i] = value
        for landed, sent, count in ((RA, a_send, plane), (RB, b_send, chips)):
            others = landed.at[pl.ds(0, count - 1)]
            pltpu.make_async_copy(others, others, sent).wait()

    portion = 4

    def combine(B, FACTORS, sol, res, OS, OR, out_sem):
        weights = [FACTORS[i] for i in range(STEPS)]
        leftover = [FACTORS[STEPS + i] for i in range(SIZE)]

        def out_copies(part):
            where = pl.ds(part * portion, portion)
            return [pltpu.make_async_copy(src.at[where], dst.at[where], out_sem.at[i, part])
                    for i, (src, dst) in enumerate(((OS, sol), (OR, res)))]

        @pl.loop(0, nx // portion)
        def _(part):
            for within in range(portion):
                x = part * portion + within
                for t in range(tiles):
                    where = pl.ds(pl.multiple_of((x + 1) * pitch + 8 + 8 * t, 8), 8)
                    values = [B[i, where, :] for i in range(SIZE)]
                    OS[x, pl.ds(8 * t, 8), :] = tree([weights[i] * values[i] for i in range(STEPS)])
                    OR[x, pl.ds(8 * t, 8), :] = tree([leftover[i] * values[i] for i in range(SIZE)])

            for copy in out_copies(part):
                copy.start()

        @pl.loop(0, nx // portion)
        def _(part):
            for copy in out_copies(part):
                copy.wait()

    results = (jax.ShapeDtypeStruct((8, (nx + 2) * pitch, LANES), F32),
               jax.ShapeDtypeStruct((MOMENTS, 8, LANES), F32))
    outs = [pltpu.VMEM((nx, ny, nz), F32), pltpu.VMEM((nx, ny, nz), F32),
            pltpu.SemaphoreType.DMA((2, nx // portion))]
    scratch = [
        pltpu.VMEM((nx, ny, nz), F32), pltpu.VMEM((nx, ny, nz), F32), pltpu.VMEM((nx, ny, nz), jnp.int32),
        pltpu.VMEM((8, 2, nx, LANES), F32), pltpu.VMEM((8, 2, nx, LANES), F32),
        pltpu.VMEM((8, halves, 8, LANES), F32), pltpu.VMEM((8, 2, halves, 8, LANES), F32),
        pltpu.VMEM(((nx + 1) * ny, LANES), F32), pltpu.VMEM(((nx + 2) * pitch, LANES), F32),
        pltpu.VMEM((2, nx, LANES), F32),
        pltpu.VMEM((nx * ny, LANES), F32), pltpu.VMEM((nx * ny, LANES), F32),
        pltpu.VMEM((halves, 8, LANES), F32), pltpu.VMEM((halves, 8, LANES), F32),
        pltpu.VMEM((nx * ny, LANES), F32),
        pltpu.VMEM((16, LANES), F32),
        pltpu.VMEM((1, LANES), F32), pltpu.VMEM((plane, 1, LANES), F32),
        pltpu.VMEM((1, LANES), F32), pltpu.VMEM((chips, 1, LANES), F32),
        pltpu.SemaphoreType.DMA((3, nx // chunk)),
    ] + [pltpu.SemaphoreType.DMA((8, 2))] * 6 + [pltpu.SemaphoreType.DMA] * 4 + [
        pltpu.SemaphoreType.REGULAR((3,))]
    return kernel, results, scratch, combine, outs


def solution(mesh):
    counts = tuple(mesh.shape[axis] for axis in ("gx", "gy", "gz"))

    def on_device(right_side, inv_density, active):
        kernel, results, scratch, combine, outs = make_kernel(right_side.shape, counts)
        whole = pl.BlockSpec(memory_space=pltpu.VMEM)
        basis, factors = pl.pallas_call(
            kernel,
            out_shape=results,
            in_specs=[pl.BlockSpec(memory_space=pltpu.HBM)] * 3,
            out_specs=(whole, whole),
            scratch_shapes=scratch,
            compiler_params=pltpu.CompilerParams(
                collective_id=0, has_side_effects=True, vmem_limit_bytes=16 << 20),
        )(*[pltpu.with_memory_space_constraint(a, pltpu.HBM) for a in (right_side, inv_density, active)])
        field = jax.ShapeDtypeStruct(right_side.shape, F32)
        return pl.pallas_call(
            combine,
            out_shape=(field, field),
            in_specs=[whole, whole],
            out_specs=(pl.BlockSpec(memory_space=pltpu.HBM),) * 2,
            scratch_shapes=outs,
            compiler_params=pltpu.CompilerParams(vmem_limit_bytes=16 << 20),
        )(basis, factors)

    placed = P("gx", "gy", "gz")
    return jax.shard_map(
        on_device, mesh=mesh, in_specs=(placed,) * 3, out_specs=(placed,) * 2, check_vma=False)
```
